128 devices in a mesh: wide: 16 (over y_lo, z, core), narrow: 8 (over x, y_hi).
Axes of the slice: x: 4, y: 4 (y_hi: 2, y_lo: 2; y = y_hi * 2 + y_lo), z: 4, core: 2. Of those that a mesh axis runs over, the one named last changes fastest.
Arguments:
- fields: float32 [5, 16, 64, 256], P(None, 'wide', 'narrow'), may hold values from -2.1 to 6.1, as said below
- prior_modes: bfloat16 [124, 5, 16, 16384], P(None, None, 'wide', 'narrow'), may hold values from -360 to 360, as said below
Outputs:
- flow_state: float32 [5, 16, 64, 256], P(None, 'wide', 'narrow')
- factor: float32 [128, 128], replicated
The draws below stay inside these ranges and needn't reach their ends.
Inputs may be any that keep to these rules, and one draw needn't show every extreme that they name: `fields`: density and pressure lie in 0.6 to 1.4, each velocity component below 1.5 in magnitude. `prior_modes`: the columns are linearly independent.
All inputs are finite; a program needn't handle non-finite values.
Results may differ from the reference program's by a relative error of at most 0.0014.
Values may be sent and summed in bfloat16 or wider, within the bound.
No kernel may reach another device: no remote copies, remote signals or barrier semaphores. Data moves between devices by JAX's collectives and lax.ppermute only.
A program may use at most 64 MiB of HBM per device.

```python
import jax
import jax.numpy as jnp
from jax import lax

COLS = 128
SNAPS = 4
STEPS = 2
PRIOR = 124
NX = 16
NY = 64
NZ = 256


GAMMA = 1.4


def base_state(key):
    key_density, key_velocity, key_pressure = jax.random.split(jax.random.fold_in(key, 101), 3)
    density = jax.random.uniform(key_density, (NX, NY, NZ), jnp.float32, 0.6, 1.4)
    velocity = 0.3 * jax.random.truncated_normal(key_velocity, -3.0, 3.0, (3, NX, NY, NZ), jnp.float32)
    pressure = jax.random.uniform(key_pressure, (NX, NY, NZ), jnp.float32, 0.6, 1.4)
    momentum = density[None] * velocity
    energy = pressure / (GAMMA - 1.0) + 0.5 * density * jnp.sum(velocity * velocity, 0)
    return jnp.concatenate([density[None], momentum, energy[None]], 0)


def bump_profile(key, length_cells):
    spread = length_cells / 8.0
    centre = jax.random.uniform(key, (PRIOR,), jnp.float32, 0.0, 1.0) * length_cells
    position = jnp.arange(length_cells, dtype=jnp.float32) + 0.5
    distance = jnp.abs(position[None, :] - centre[:, None])
    distance = jnp.minimum(distance, length_cells - distance)
    scaled = distance / spread
    return jnp.exp(-0.5 * scaled * scaled)


def draw_fields(key, part):
    return base_state(key)


def draw_prior_modes(key, part):
    state_base = jnp.swapaxes(base_state(key), 2, 3)
    coefficients = jax.random.uniform(jax.random.fold_in(key, 202), (PRIOR,), jnp.float32, -1.0, 1.0)
    scales = jnp.exp(jax.random.uniform(jax.random.fold_in(key, 212), (PRIOR,), jnp.float32, jnp.log(0.2), jnp.log(2.0)))
    bump_x = bump_profile(jax.random.fold_in(key, 222), NX)
    bump_y = bump_profile(jax.random.fold_in(key, 232), NY)
    bump_z = bump_profile(jax.random.fold_in(key, 242), NZ)
    envelope = 1.0 + 7.0 * bump_x[:, :, None, None] * bump_z[:, None, :, None] * bump_y[:, None, None, :]
    disorder = jax.random.truncated_normal(jax.random.fold_in(key, 303), -4.0, 4.0, (PRIOR, 5, NX, NZ, NY), jnp.float32)
    columns_all = scales[:, None, None, None, None] * envelope[:, None] * (coefficients[:, None, None, None, None] * state_base[None] + disorder)
    return columns_all.reshape(PRIOR, 5, NX, NZ * NY).astype(jnp.bfloat16)


def setup_inputs(seed: int = 0) -> dict:
    seeds = jax.random.split(jax.random.key(seed), 3)
    return {
        "fields": draw_fields(jax.random.fold_in(seeds[2], 71), 0),
        "prior_modes": draw_prior_modes(jax.random.fold_in(seeds[2], 71), 0),
    }


GAMMA = 1.4
TIME_STEP = 0.25
VISCOSITY = 0.15

def flux_of(current, dim_index):
    density = current[0]
    momentum = current[1:4]
    energy = current[4]
    vel_d = momentum[dim_index] / density
    pressure = (GAMMA - 1.0) * (energy - 0.5 * (momentum[0] * momentum[0] + momentum[1] * momentum[1] + momentum[2] * momentum[2]) / density)
    components = [momentum[dim_index], momentum[0] * vel_d, momentum[1] * vel_d, momentum[2] * vel_d, (energy + pressure) * vel_d]
    components[1 + dim_index] = components[1 + dim_index] + pressure
    return jnp.stack(components)

def tendency(current):
    flux_x = flux_of(current, 0)
    flux_y = flux_of(current, 1)
    flux_z = flux_of(current, 2)
    divergence = jnp.roll(flux_x, -1, 1) - jnp.roll(flux_x, 1, 1) + (jnp.roll(flux_y, -1, 2) - jnp.roll(flux_y, 1, 2)) + (jnp.roll(flux_z, -1, 3) - jnp.roll(flux_z, 1, 3))
    laplace = jnp.roll(current, -1, 1) + jnp.roll(current, 1, 1) + jnp.roll(current, -1, 2) + jnp.roll(current, 1, 2) + jnp.roll(current, -1, 3) + jnp.roll(current, 1, 3) - 6.0 * current
    return -0.5 * divergence + VISCOSITY * laplace

def reference(fields, prior_modes):
    current = fields
    snapshots = []
    for step_index in range(STEPS):
        section_one = current + TIME_STEP * tendency(current)
        snapshots.append(section_one.astype(jnp.bfloat16))
        current = 0.5 * current + 0.5 * (section_one + TIME_STEP * tendency(section_one))
        snapshots.append(current.astype(jnp.bfloat16))
    snap_stack = jnp.swapaxes(jnp.stack(snapshots), 3, 4).reshape(SNAPS, 5, NX, NZ * NY)

    def accumulate(x_index, gram_total):
        basis_rows = lax.dynamic_index_in_dim(prior_modes, x_index, 2, keepdims=False).reshape(PRIOR, -1).astype(jnp.float32)
        snap_rows = lax.dynamic_index_in_dim(snap_stack, x_index, 2, keepdims=False).reshape(SNAPS, -1).astype(jnp.float32)
        stacked = jnp.concatenate([basis_rows, snap_rows], 0)
        return gram_total + jnp.dot(stacked, stacked.T, precision=lax.Precision.HIGHEST)
    gram_total = lax.fori_loop(0, NX, accumulate, jnp.zeros((COLS, COLS), jnp.float32))
    gram_total = gram_total * (1.0 / (NX * NY * NZ))
    factor = jnp.linalg.cholesky(gram_total).T
    return (current, factor)
```

```python
import jax
import jax.numpy as jnp
from jax import lax
from jax.sharding import PartitionSpec as P

STEPS = 2


GAMMA = 1.4
TIME_STEP = 0.25
VISCOSITY = 0.15


def extended(block, sides, width):
    for axis, dim in sides:
        count = lax.axis_size(axis)
        forward = [(i, i + 1) for i in range(count - 1)]
        forward.append((count - 1, 0))
        backward = [(target, source) for source, target in forward]
        low = lax.ppermute(
            lax.slice_in_dim(block, block.shape[dim] - width, None, axis=dim), axis, forward
        )
        high = lax.ppermute(lax.slice_in_dim(block, 0, width, axis=dim), axis, backward)
        block = jnp.concatenate([low, block, high], axis=dim)
    return block


def flux_of(current, dim_index):
    density = current[0]
    momentum = current[1:4]
    energy = current[4]
    vel_d = momentum[dim_index] / density
    pressure = (GAMMA - 1.0) * (
        energy
        - 0.5
        * (momentum[0] * momentum[0] + momentum[1] * momentum[1] + momentum[2] * momentum[2])
        / density
    )
    components = [
        momentum[dim_index],
        momentum[0] * vel_d,
        momentum[1] * vel_d,
        momentum[2] * vel_d,
        (energy + pressure) * vel_d,
    ]
    components[1 + dim_index] = components[1 + dim_index] + pressure
    return jnp.stack(components)


def tendency(current):
    padded = extended(current.astype(jnp.bfloat16), (("wide", 1), ("narrow", 2)), 1).astype(
        current.dtype
    )
    flux_x = flux_of(padded[:, :, 1:-1], 0)
    flux_y = flux_of(padded[:, 1:-1, :], 1)
    flux_z = flux_of(current, 2)
    divergence = (
        flux_x[:, 2:]
        - flux_x[:, :-2]
        + (flux_y[:, :, 2:] - flux_y[:, :, :-2])
        + (jnp.roll(flux_z, -1, 3) - jnp.roll(flux_z, 1, 3))
    )
    laplace = (
        padded[:, 2:, 1:-1]
        + padded[:, :-2, 1:-1]
        + padded[:, 1:-1, 2:]
        + padded[:, 1:-1, :-2]
        + jnp.roll(current, -1, 3)
        + jnp.roll(current, 1, 3)
        - 6.0 * current
    )
    return -0.5 * divergence + VISCOSITY * laplace


def local(fields, prior_modes):
    wide_count = lax.axis_size("wide")
    narrow_count = lax.axis_size("narrow")
    cells_x, cells_y, cells_z = (fields.shape[1], fields.shape[2], fields.shape[3])
    inverse_cells = 1.0 / (cells_x * wide_count * cells_y * narrow_count * cells_z)
    flat_modes = prior_modes.reshape(prior_modes.shape[0], -1)
    contract = (((1,), (1,)), ((), ()))
    gram_modes = lax.dot_general(
        flat_modes, flat_modes, contract, preferred_element_type=jnp.float32
    )
    current = fields
    snapshots = []
    for step_index in range(STEPS):
        section_one = current + TIME_STEP * tendency(current)
        snapshots.append(section_one.astype(jnp.bfloat16))
        current = 0.5 * current + 0.5 * (section_one + TIME_STEP * tendency(section_one))
        snapshots.append(current.astype(jnp.bfloat16))
    arrived = lax.all_to_all(
        jnp.stack(snapshots), "narrow", split_axis=4, concat_axis=3, tiled=True
    )
    snap_rows = jnp.swapaxes(arrived, 3, 4).reshape(arrived.shape[0], -1)
    cross_gram = lax.dot_general(
        flat_modes, snap_rows, contract, preferred_element_type=jnp.float32
    )
    snap_gram = lax.dot_general(snap_rows, snap_rows, contract, preferred_element_type=jnp.float32)
    gram_local = jnp.concatenate(
        [
            jnp.concatenate([gram_modes, cross_gram], 1),
            jnp.concatenate([cross_gram.T, snap_gram], 1),
        ],
        0,
    )
    gram_local = gram_local * inverse_cells
    devices = wide_count * narrow_count
    everywhere = ("wide", "narrow")
    pieces = gram_local.reshape(devices, 1, -1)
    pieces = lax.all_to_all(pieces, everywhere, split_axis=0, concat_axis=0, tiled=True)
    piece = jnp.sum(pieces, axis=0, keepdims=True)
    copies = jnp.broadcast_to(piece, pieces.shape)
    copies = lax.all_to_all(copies, everywhere, split_axis=0, concat_axis=0, tiled=True)
    gram_whole = copies.reshape(gram_local.shape)
    factor = jnp.linalg.cholesky(gram_whole).T
    return (current, factor)


def solution(mesh):
    placed = (P(None, "wide", "narrow", None), P(None, None, "wide", "narrow"))
    return jax.shard_map(
        local,
        mesh=mesh,
        in_specs=placed,
        out_specs=(P(None, "wide", "narrow", None), P()),
        check_vma=False,
    )
```

```python
import functools

import jax
import jax.numpy as jnp
from jax import lax
from jax.experimental import pallas as pl
from jax.experimental.pallas import tpu as pltpu
from jax.sharding import PartitionSpec as P

GAMMA = 1.4
TIME_STEP = 0.25
VISCOSITY = 0.15
MEANS = (1.0, 0.0, 0.0, 0.0, 2.5)
HALO = 4
WIDE = 16
NARROW = 8
DEVICES = WIDE * NARROW
MODES = 124
COLS = 128
ZPART = 32
WINDOW = ZPART + 2 * HALO
YPART = 8
NY = 64
INVERSE_CELLS = 1.0 / 262144.0
EVERYWHERE = ("wide", "narrow")
F32 = jnp.float32
BF16 = jnp.bfloat16


def lanes(shape):
    return lax.broadcasted_iota(jnp.int32, shape, len(shape) - 1)


def pack_kernel(fields_ref, modes_ref, out_ref, gram_ref):
    comp = pl.program_id(0)
    block = modes_ref[0]
    product = lax.dot_general(
        block, block, (((1,), (1,)), ((), ())), preferred_element_type=F32
    )

    @pl.when(comp == 0)
    def _():
        gram_ref[...] = jnp.zeros_like(gram_ref)

    gram_ref[0:MODES, 0:MODES] += product

    @pl.when(comp == pl.num_programs(0) - 1)
    def _():
        gram = gram_ref[...]
        high = gram.astype(BF16).astype(F32)
        rest = gram - high
        middle = rest.astype(BF16).astype(F32)
        low = rest - middle
        lane = lanes((YPART, 128))
        lane_full = lanes((COLS, 128))
        shifted = [fields_ref[c] - MEANS[c] for c in range(5)]
        for n in range(NARROW):
            def window(c, place):
                amount = (place * WINDOW + HALO - ZPART * n) % 256
                moved = pltpu.roll(shifted[c], amount, 1) if amount else shifted[c]
                return moved[:, 0:128]

            first = jnp.where(
                lane < WINDOW,
                window(0, 0),
                jnp.where(lane < 2 * WINDOW, window(1, 1), window(2, 2)),
            )
            first = jnp.where(lane < 3 * WINDOW, first, 0.0)
            second = jnp.where(lane < WINDOW, window(3, 0), window(4, 1))

            def turned(x, place):
                amount = (place - 16 * n) % 128
                return pltpu.roll(x, amount, 1) if amount else x

            parts = jnp.where(
                lane_full < 96,
                turned(high, 80),
                jnp.where(lane_full < 112, turned(middle, 96), turned(low, 112)),
            ).reshape(WIDE, YPART, 128)
            lower = jnp.broadcast_to(first[None], (WIDE, YPART, 128))
            upper = jnp.where(lane[None] < 2 * WINDOW, second[None], parts)
            piece = jnp.concatenate([lower, upper], axis=1).astype(BF16)
            out_ref[:, n] = piece


def pack(fields, modes):
    return pl.pallas_call(
        pack_kernel,
        grid=(5,),
        in_specs=[
            pl.BlockSpec((5, YPART, 256), lambda c: (0, 0, 0)),
            pl.BlockSpec((1, MODES, 2048), lambda c: (c, 0, 0)),
        ],
        out_specs=pl.BlockSpec((WIDE, NARROW, 16, 128), lambda c: (0, 0, 0, 0)),
        out_shape=jax.ShapeDtypeStruct((WIDE, NARROW, 16, 128), BF16),
        scratch_shapes=[pltpu.VMEM((COLS, 128), F32)],
        name="pack",
    )(fields, modes)


def up(x, axis):
    return pltpu.roll(x, x.shape[axis] - 1, axis)


def down(x, axis):
    return pltpu.roll(x, 1, axis)


def fluxes(u, directions):
    density, m1, m2, m3, energy = u
    inverse = 1.0 / density
    v = (m1 * inverse, m2 * inverse, m3 * inverse)
    products = {}
    momenta = (m1, m2, m3)
    for i in range(3):
        products[(i, i)] = momenta[i] * v[i]
    pressure = (GAMMA - 1.0) * (
        energy - 0.5 * (products[(0, 0)] + products[(1, 1)] + products[(2, 2)])
    )
    total = energy + pressure
    out = []
    for d in directions:
        row = [momenta[d]]
        for i in range(3):
            if i == d:
                row.append(products[(d, d)] + pressure)
            else:
                key = (min(i, d), max(i, d))
                if key not in products:
                    products[key] = momenta[key[0]] * v[key[1]]
                row.append(products[key])
        row.append(total * v[d])
        out.append(row)
    return out


def section(load, planes):
    ahead, behind, partial = {}, {}, {}
    centre = 1.0 - 6.0 * VISCOSITY * TIME_STEP
    soft = VISCOSITY * TIME_STEP
    half = 0.5 * TIME_STEP
    wanted = set(planes)
    everything = sorted({p + s for p in planes for s in (-1, 0, 1)})
    result = {}
    for p in everything:
        u = load(p)
        inner = p in wanted
        rows = fluxes(u, (0, 1, 2) if inner else (0,))
        smooth = [soft * x for x in u]
        ahead[p] = [smooth[c] - half * rows[0][c] for c in range(5)]
        behind[p] = [smooth[c] + half * rows[0][c] for c in range(5)]
        if inner:
            total = []
            for c in range(5):
                y, z = half * rows[1][c], half * rows[2][c]
                total.append(
                    centre * u[c]
                    + (up(smooth[c] - y, 0) + down(smooth[c] + y, 0))
                    + (up(smooth[c] - z, 1) + down(smooth[c] + z, 1))
                )
            partial[p] = total
        q = p - 1
        if q in wanted:
            result[q] = [partial[q][c] + (ahead[q + 1][c] + behind[q - 1][c]) for c in range(5)]
            yield q, result[q]


def step_kernel(w_ref, recv_ref, modes_hbm, whole_ref, back_ref, one, two, modes_ref, turn_ref, sem):
    copies = [
        pltpu.make_async_copy(modes_hbm.at[c], modes_ref.at[c], sem.at[c]) for c in range(5)
    ]
    for copy in copies:
        copy.start()
    w = w_ref[0]
    lane = lanes((NY, 128))

    def load(p):
        start = lax.rem(w + (p + WIDE), WIDE) * NARROW
        block = recv_ref[pl.ds(start, NARROW)].astype(F32)
        lower = block[:, 0:8].reshape(NY, 128)
        upper = block[:, 8:16].reshape(NY, 128)
        return [
            lower + MEANS[0],
            pltpu.roll(lower, 128 - WINDOW, 1),
            pltpu.roll(lower, 128 - 2 * WINDOW, 1),
            upper,
            pltpu.roll(upper, 128 - WINDOW, 1) + MEANS[4],
        ]

    terms = recv_ref[:, 8:16, :].astype(F32)
    summed = jnp.sum(terms, axis=0)
    block = (pltpu.roll(summed, 16, 1) + pltpu.roll(summed, 32, 1)) + pltpu.roll(summed, 48, 1)

    packed = [jnp.zeros((NY, 128), F32) for _ in range(5)]
    valid = lane < ZPART

    def keep(index, u):
        for c in range(5):
            value = pltpu.roll(u[c], 128 - HALO, 1) if index == 0 else pltpu.roll(
                u[c], ZPART * index - HALO, 1
            )
            inside = (lane >= ZPART * index) & (lane < ZPART * (index + 1))
            packed[c] = jnp.where(inside, value, packed[c])

    def stored(ref, offset):
        return lambda p: [ref[p + offset, c] for c in range(5)]

    for q, v in section(load, range(-3, 4)):
        for c in range(5):
            one[q + 3, c] = v[c]
        if q == 0:
            keep(0, v)
    for q, v in section(stored(one, 3), range(-2, 3)):
        u = load(q)
        new = [0.5 * (u[c] + v[c]) for c in range(5)]
        for c in range(5):
            two[q + 2, c] = new[c]
        if q == 0:
            keep(1, new)
    for q, v in section(stored(two, 2), range(-1, 2)):
        for c in range(5):
            one[q + 1, c] = v[c]
        if q == 0:
            keep(2, v)
    for q, v in section(stored(one, 1), range(0, 1)):
        new = [0.5 * (two[2, c] + v[c]) for c in range(5)]
        keep(3, new)
        back = [None] * 5
        spread = jnp.zeros((NY, 128), F32)
        for c in range(4):
            value = pltpu.roll(new[c], 128 - HALO, 1) if c == 0 else pltpu.roll(
                new[c], ZPART * c - HALO, 1
            )
            inside = (lane >= ZPART * c) & (lane < ZPART * (c + 1))
            spread = jnp.where(inside, value, spread)
        last = jnp.where(valid, pltpu.roll(new[4], 128 - HALO, 1), 0.0)
        back_ref[:, 0:8, :] = spread.reshape(NARROW, YPART, 128)
        back_ref[:, 8:16, :] = last.reshape(NARROW, YPART, 128)

    cross = jnp.zeros((4, MODES), F32)
    square = jnp.zeros((4, 4), F32)
    contract = (((1,), (1,)), ((), ()))
    for c in range(5):
        rounded = packed[c].astype(BF16).astype(F32)
        pair = jnp.concatenate([rounded, pltpu.roll(rounded, 127, 1)], axis=0)
        turn_ref[c] = pair.T
    for c in range(5):
        chunks = [turn_ref[c, pl.ds(2 * k, 4, stride=ZPART), :] for k in range(16)]
        rows = jnp.concatenate(chunks, axis=1).astype(BF16)
        copies[c].wait()
        cross += lax.dot_general(rows, modes_ref[c], contract, preferred_element_type=F32)
        square += lax.dot_general(rows, rows, contract, preferred_element_type=F32)
    top = jnp.concatenate([cross, square], axis=1)
    lane8 = lanes((4, 128))
    bottom = jnp.where(lane8 < 16, block[0:4], pltpu.roll(block, 16, 1)[4:8])
    bottom = jnp.where(lane8 < 32, bottom, 0.0)
    piece = jnp.concatenate([top, bottom], axis=0) * INVERSE_CELLS
    whole_ref[...] = jnp.broadcast_to(piece[None], whole_ref.shape)


def steps(w, recv, modes):
    return pl.pallas_call(
        step_kernel,
        in_specs=[
            pl.BlockSpec(memory_space=pltpu.SMEM),
            pl.BlockSpec(memory_space=pltpu.VMEM),
            pl.BlockSpec(memory_space=pl.ANY),
        ],
        out_specs=[
            pl.BlockSpec(memory_space=pltpu.VMEM),
            pl.BlockSpec(memory_space=pltpu.VMEM),
        ],
        out_shape=[
            jax.ShapeDtypeStruct((DEVICES, 8, 128), F32),
            jax.ShapeDtypeStruct((NARROW, 16, 128), F32),
        ],
        scratch_shapes=[
            pltpu.VMEM((7, 5, NY, 128), F32),
            pltpu.VMEM((5, 5, NY, 128), F32),
            pltpu.VMEM((5, MODES, 2048), BF16),
            pltpu.VMEM((5, 128, 128), F32),
            pltpu.SemaphoreType.DMA((5,)),
        ],
        name="steps",
    )(w, recv, modes)


def gram_kernel(whole_ref, gram_ref):
    cross = jnp.sum(whole_ref[:, 0:4, :], axis=0)
    lane = lanes((4, 128))
    for a in range(16):
        low = jnp.zeros((4, 128), F32)
        high = jnp.zeros((4, 128), F32)
        for b in range(8):
            part = whole_ref[8 * a + b, 4:8, :]
            inside = (lane >= 16 * b) & (lane < 16 * (b + 1))
            first = pltpu.roll(part, 16 * b, 1) if b else part
            second = pltpu.roll(part, (16 * b - 16) % 128, 1) if b != 1 else part
            low = jnp.where(inside, first, low)
            high = jnp.where(inside, second, high)
        if a == 15:
            high = cross
        gram_ref[8 * a : 8 * a + 8, :] = jnp.concatenate([low, high], axis=0)


def gather_gram(whole):
    return pl.pallas_call(
        gram_kernel,
        out_shape=jax.ShapeDtypeStruct((COLS, 128), F32),
        name="gram",
    )(whole)


def owner_kernel(back_ref, out_ref):
    lane = lanes((YPART, 256))
    for c in range(5):
        total = jnp.zeros((YPART, 256), F32)
        place = ZPART * (c % 4)
        row = 8 * (c // 4)
        for n in range(NARROW):
            part = back_ref[n, row : row + 8, :]
            part = jnp.concatenate([part, part], axis=1)
            amount = (ZPART * n - place) % 256
            part = pltpu.roll(part, amount, 1) if amount else part
            inside = (lane >= ZPART * n) & (lane < ZPART * (n + 1))
            total = jnp.where(inside, part, total)
        out_ref[c] = total


def owner(back):
    return pl.pallas_call(
        owner_kernel,
        out_shape=jax.ShapeDtypeStruct((5, YPART, 256), F32),
        name="owner",
    )(back)


def local(fields, prior_modes):
    modes = jnp.transpose(prior_modes[:, :, 0, :], (1, 0, 2))
    w = lax.axis_index("wide").astype(jnp.int32).reshape(1)
    sent = pack(fields[:, 0], modes).reshape(DEVICES, 16, 128)
    recv = lax.all_to_all(sent, EVERYWHERE, split_axis=0, concat_axis=0, tiled=True)
    whole, back = steps(w, recv, modes)
    whole = lax.all_to_all(whole, EVERYWHERE, split_axis=0, concat_axis=0, tiled=True)
    back = lax.all_to_all(back, "narrow", split_axis=0, concat_axis=0, tiled=True)
    state = owner(back)[:, None]
    gram = gather_gram(whole)
    factor = jnp.linalg.cholesky(gram, symmetrize_input=False).T
    return (state, factor)


def solution(mesh):
    placed = (P(None, "wide", "narrow", None), P(None, None, "wide", "narrow"))
    return jax.shard_map(
        local,
        mesh=mesh,
        in_specs=placed,
        out_specs=(P(None, "wide", "narrow", None), P()),
        check_vma=False,
    )
```

```python
import jax
import jax.numpy as jnp
from jax import lax
from jax.experimental import pallas as pl
from jax.experimental.pallas import tpu as pltpu
from jax.sharding import PartitionSpec as P


GAMMA = 1.4
TIME_STEP = 0.25
VISCOSITY = 0.15
MEANS = (1.0, 0.0, 0.0, 0.0, 2.5)
HALO = 4
WIDE = 16
NARROW = 8
DEVICES = WIDE * NARROW
MODES = 124
COLS = 128
ZPART = 32
WINDOW = ZPART + 2 * HALO
YPART = 8
NY = 64
INVERSE_CELLS = 1.0 / 262144.0
EVERYWHERE = ("wide", "narrow")
F32 = jnp.float32
BF16 = jnp.bfloat16


def lanes(shape):
    return lax.broadcasted_iota(jnp.int32, shape, len(shape) - 1)


def pack_kernel(fields_ref, modes_ref, out_ref, gram_ref):
    comp = pl.program_id(0)
    block = modes_ref[0]
    product = lax.dot_general(
        block, block, (((1,), (1,)), ((), ())), preferred_element_type=F32
    )

    @pl.when(comp == 0)
    def _():
        gram_ref[...] = jnp.zeros_like(gram_ref)

    gram_ref[0:MODES, 0:MODES] += product

    @pl.when(comp == pl.num_programs(0) - 1)
    def _():
        gram = gram_ref[...]
        high = gram.astype(BF16).astype(F32)
        rest = gram - high
        middle = rest.astype(BF16).astype(F32)
        low = rest - middle
        lane = lanes((YPART, 128))
        lane_full = lanes((COLS, 128))
        shifted = [fields_ref[c] - MEANS[c] for c in range(5)]
        for n in range(NARROW):
            def window(c, place):
                amount = (place * WINDOW + HALO - ZPART * n) % 256
                moved = pltpu.roll(shifted[c], amount, 1) if amount else shifted[c]
                return moved[:, 0:128]

            first = jnp.where(
                lane < WINDOW,
                window(0, 0),
                jnp.where(lane < 2 * WINDOW, window(1, 1), window(2, 2)),
            )
            first = jnp.where(lane < 3 * WINDOW, first, 0.0)
            second = jnp.where(lane < WINDOW, window(3, 0), window(4, 1))

            def turned(x, place):
                amount = (place - 16 * n) % 128
                return pltpu.roll(x, amount, 1) if amount else x

            parts = jnp.where(
                lane_full < 96,
                turned(high, 80),
                jnp.where(lane_full < 112, turned(middle, 96), turned(low, 112)),
            ).reshape(WIDE, YPART, 128)
            lower = jnp.broadcast_to(first[None], (WIDE, YPART, 128))
            upper = jnp.where(lane[None] < 2 * WINDOW, second[None], parts)
            piece = jnp.concatenate([lower, upper], axis=1).astype(BF16)
            out_ref[:, n] = piece


def pack(fields, modes):
    return pl.pallas_call(
        pack_kernel,
        grid=(5,),
        in_specs=[
            pl.BlockSpec((5, YPART, 256), lambda c: (0, 0, 0)),
            pl.BlockSpec((1, MODES, 2048), lambda c: (c, 0, 0)),
        ],
        out_specs=pl.BlockSpec((WIDE, NARROW, 16, 128), lambda c: (0, 0, 0, 0)),
        out_shape=jax.ShapeDtypeStruct((WIDE, NARROW, 16, 128), BF16),
        scratch_shapes=[pltpu.VMEM((COLS, 128), F32)],
        name="pack",
        compiler_params=pltpu.CompilerParams(vmem_limit_bytes=16 * 2**20),
    )(fields, modes)


def up(x, axis):
    return pltpu.roll(x, x.shape[axis] - 1, axis)


def down(x, axis):
    return pltpu.roll(x, 1, axis)


def fluxes(u, directions):
    density, m1, m2, m3, energy = u
    inverse = 1.0 / density
    v = (m1 * inverse, m2 * inverse, m3 * inverse)
    products = {}
    momenta = (m1, m2, m3)
    for i in range(3):
        products[(i, i)] = momenta[i] * v[i]
    pressure = (GAMMA - 1.0) * (
        energy - 0.5 * (products[(0, 0)] + products[(1, 1)] + products[(2, 2)])
    )
    total = energy + pressure
    out = []
    for d in directions:
        row = [momenta[d]]
        for i in range(3):
            if i == d:
                row.append(products[(d, d)] + pressure)
            else:
                key = (min(i, d), max(i, d))
                if key not in products:
                    products[key] = momenta[key[0]] * v[key[1]]
                row.append(products[key])
        row.append(total * v[d])
        out.append(row)
    return out


def section(load, planes):
    ahead, behind, partial = {}, {}, {}
    centre = 1.0 - 6.0 * VISCOSITY * TIME_STEP
    soft = VISCOSITY * TIME_STEP
    half = 0.5 * TIME_STEP
    wanted = set(planes)
    everything = sorted({p + s for p in planes for s in (-1, 0, 1)})
    result = {}
    for p in everything:
        u = load(p)
        inner = p in wanted
        rows = fluxes(u, (0, 1, 2) if inner else (0,))
        smooth = [soft * x for x in u]
        ahead[p] = [smooth[c] - half * rows[0][c] for c in range(5)]
        behind[p] = [smooth[c] + half * rows[0][c] for c in range(5)]
        if inner:
            total = []
            for c in range(5):
                y, z = half * rows[1][c], half * rows[2][c]
                total.append(
                    centre * u[c]
                    + (up(smooth[c] - y, 0) + down(smooth[c] + y, 0))
                    + (up(smooth[c] - z, 1) + down(smooth[c] + z, 1))
                )
            partial[p] = total
        q = p - 1
        if q in wanted:
            result[q] = [partial[q][c] + (ahead[q + 1][c] + behind[q - 1][c]) for c in range(5)]
            yield q, result[q]


def step_kernel(w_ref, recv_ref, modes_hbm, whole_ref, back_ref, one, two, modes_ref, turn_ref, sem):
    copies = [
        pltpu.make_async_copy(modes_hbm.at[c], modes_ref.at[c], sem.at[c]) for c in range(5)
    ]
    for copy in copies:
        copy.start()
    w = w_ref[0]
    lane = lanes((NY, 128))

    def load(p):
        start = lax.rem(w + (p + WIDE), WIDE) * NARROW
        block = recv_ref[pl.ds(start, NARROW)].astype(F32)
        lower = block[:, 0:8].reshape(NY, 128)
        upper = block[:, 8:16].reshape(NY, 128)
        return [
            lower + MEANS[0],
            pltpu.roll(lower, 128 - WINDOW, 1),
            pltpu.roll(lower, 128 - 2 * WINDOW, 1),
            upper,
            pltpu.roll(upper, 128 - WINDOW, 1) + MEANS[4],
        ]

    terms = recv_ref[:, 8:16, :].astype(F32)
    summed = jnp.sum(terms, axis=0)
    block = (pltpu.roll(summed, 16, 1) + pltpu.roll(summed, 32, 1)) + pltpu.roll(summed, 48, 1)

    packed = [jnp.zeros((NY, 128), F32) for _ in range(5)]
    valid = lane < ZPART

    def keep(index, u):
        for c in range(5):
            value = pltpu.roll(u[c], 128 - HALO, 1) if index == 0 else pltpu.roll(
                u[c], ZPART * index - HALO, 1
            )
            inside = (lane >= ZPART * index) & (lane < ZPART * (index + 1))
            packed[c] = jnp.where(inside, value, packed[c])

    def stored(ref, offset):
        return lambda p: [ref[p + offset, c] for c in range(5)]

    for q, v in section(load, range(-3, 4)):
        for c in range(5):
            one[q + 3, c] = v[c]
        if q == 0:
            keep(0, v)
    for q, v in section(stored(one, 3), range(-2, 3)):
        u = load(q)
        new = [0.5 * (u[c] + v[c]) for c in range(5)]
        for c in range(5):
            two[q + 2, c] = new[c]
        if q == 0:
            keep(1, new)
    for q, v in section(stored(two, 2), range(-1, 2)):
        for c in range(5):
            one[q + 1, c] = v[c]
        if q == 0:
            keep(2, v)
    for q, v in section(stored(one, 1), range(0, 1)):
        new = [0.5 * (two[2, c] + v[c]) for c in range(5)]
        keep(3, new)
        spread = jnp.zeros((NY, 128), F32)
        for c in range(4):
            value = pltpu.roll(new[c], 128 - HALO, 1) if c == 0 else pltpu.roll(
                new[c], ZPART * c - HALO, 1
            )
            inside = (lane >= ZPART * c) & (lane < ZPART * (c + 1))
            spread = jnp.where(inside, value, spread)
        last = jnp.where(valid, pltpu.roll(new[4], 128 - HALO, 1), 0.0)
        back_ref[:, 0:8, :] = spread.reshape(NARROW, YPART, 128)
        back_ref[:, 8:16, :] = last.reshape(NARROW, YPART, 128)

    cross = jnp.zeros((4, MODES), F32)
    square = jnp.zeros((4, 4), F32)
    contract = (((1,), (1,)), ((), ()))
    for c in range(5):
        rounded = packed[c].astype(BF16).astype(F32)
        pair = jnp.concatenate([rounded, pltpu.roll(rounded, 127, 1)], axis=0)
        turn_ref[c] = pair.T
    for c in range(5):
        chunks = [turn_ref[c, pl.ds(2 * k, 4, stride=ZPART), :] for k in range(16)]
        rows = jnp.concatenate(chunks, axis=1).astype(BF16)
        copies[c].wait()
        cross += lax.dot_general(rows, modes_ref[c], contract, preferred_element_type=F32)
        square += lax.dot_general(rows, rows, contract, preferred_element_type=F32)
    top = jnp.concatenate([cross, square], axis=1)
    lane8 = lanes((4, 128))
    bottom = jnp.where(lane8 < 16, block[0:4], pltpu.roll(block, 16, 1)[4:8])
    bottom = jnp.where(lane8 < 32, bottom, 0.0)
    piece = jnp.concatenate([top, bottom], axis=0) * INVERSE_CELLS
    whole_ref[...] = jnp.broadcast_to(piece[None], whole_ref.shape)


def steps(w, recv, modes):
    return pl.pallas_call(
        step_kernel,
        in_specs=[
            pl.BlockSpec(memory_space=pltpu.SMEM),
            pl.BlockSpec(memory_space=pltpu.VMEM),
            pl.BlockSpec(memory_space=pl.ANY),
        ],
        out_specs=[
            pl.BlockSpec(memory_space=pltpu.VMEM),
            pl.BlockSpec(memory_space=pltpu.VMEM),
        ],
        out_shape=[
            jax.ShapeDtypeStruct((DEVICES, 8, 128), F32),
            jax.ShapeDtypeStruct((NARROW, 16, 128), F32),
        ],
        scratch_shapes=[
            pltpu.VMEM((7, 5, NY, 128), F32),
            pltpu.VMEM((5, 5, NY, 128), F32),
            pltpu.VMEM((5, MODES, 2048), BF16),
            pltpu.VMEM((5, 128, 128), F32),
            pltpu.SemaphoreType.DMA((5,)),
        ],
        name="steps",
        compiler_params=pltpu.CompilerParams(vmem_limit_bytes=24 * 2**20),
    )(w, recv, modes)


def along_lanes(x, j):
    return jnp.broadcast_to(x[:, j : j + 1], x.shape)


def along_rows(x, i):
    return jnp.broadcast_to(x[i : i + 1, :], x.shape)


def factor_rows(panels):
    panels = list(panels)
    lane = lanes((8, 128))
    row = lax.broadcasted_iota(jnp.int32, (8, 128), 0)
    count = len(panels)
    done = []
    for k in range(count):
        base = 8 * k
        later = range(k + 1, count)
        columns = [along_lanes(panels[k], base + j) for j in range(8)]
        rows = [along_rows(panels[k], i) for i in range(8)]
        below = {q: [along_lanes(panels[q], base + j) for j in range(8)] for q in later}
        scaled = []
        out = jnp.zeros((8, 128), F32)
        for i in range(8):
            pivot = along_rows(columns[i], i)
            inverse = 1.0 / pivot
            for j in range(i + 1, 8):
                weight = along_rows(columns[j], i) * inverse
                columns[j] = columns[j] - columns[i] * weight
                rows[j] = rows[j] - rows[i] * weight
                for q in later:
                    below[q][j] = below[q][j] - below[q][i] * weight
            scaled.append(rows[i] * inverse)
            out = jnp.where(row == i, rows[i] * lax.rsqrt(pivot), out)
        done.append(jnp.where(lane >= row + base, out, 0.0))
        for q in later:
            change = [below[q][i] * scaled[i] for i in range(8)]
            while len(change) > 1:
                change = [change[t] + change[t + 1] for t in range(0, len(change), 2)]
            panels[q] = panels[q] - change[0]
    return done


def gram_kernel(whole_ref, gram_ref):
    cross = jnp.sum(whole_ref[:, 0:4, :], axis=0)
    lane = lanes((4, 128))
    panels = []
    for a in range(16):
        low = jnp.zeros((4, 128), F32)
        high = jnp.zeros((4, 128), F32)
        for b in range(8):
            part = whole_ref[8 * a + b, 4:8, :]
            inside = (lane >= 16 * b) & (lane < 16 * (b + 1))
            first = pltpu.roll(part, 16 * b, 1) if b else part
            second = pltpu.roll(part, (16 * b - 16) % 128, 1) if b != 1 else part
            low = jnp.where(inside, first, low)
            high = jnp.where(inside, second, high)
        if a == 15:
            high = cross
        panels.append(jnp.concatenate([low, high], axis=0))
    turned = jnp.concatenate([panels[15]] * 16, axis=0).T
    lane8 = lanes((8, 128))
    for a in range(16):
        rows = turned[8 * a : 8 * a + 8]
        panels[a] = jnp.where(lane8 >= MODES, rows, panels[a])
    for a, rows in enumerate(factor_rows(panels)):
        gram_ref[8 * a : 8 * a + 8, :] = rows


def gather_gram(whole):
    return pl.pallas_call(
        gram_kernel,
        out_shape=jax.ShapeDtypeStruct((COLS, 128), F32),
        name="gram",
        compiler_params=pltpu.CompilerParams(vmem_limit_bytes=16 * 2**20),
    )(whole)


def owner_kernel(back_ref, out_ref):
    lane = lanes((YPART, 256))
    for c in range(5):
        total = jnp.zeros((YPART, 256), F32)
        place = ZPART * (c % 4)
        row = 8 * (c // 4)
        for n in range(NARROW):
            part = back_ref[n, row : row + 8, :]
            part = jnp.concatenate([part, part], axis=1)
            amount = (ZPART * n - place) % 256
            part = pltpu.roll(part, amount, 1) if amount else part
            inside = (lane >= ZPART * n) & (lane < ZPART * (n + 1))
            total = jnp.where(inside, part, total)
        out_ref[c] = total


def owner(back):
    return pl.pallas_call(
        owner_kernel,
        out_shape=jax.ShapeDtypeStruct((5, YPART, 256), F32),
        name="owner",
        compiler_params=pltpu.CompilerParams(vmem_limit_bytes=16 * 2**20),
    )(back)


def local(fields, prior_modes):
    modes = jnp.transpose(prior_modes[:, :, 0, :], (1, 0, 2))
    w = lax.axis_index("wide").astype(jnp.int32).reshape(1)
    sent = pack(fields[:, 0], modes).reshape(DEVICES, 16, 128)
    recv = lax.all_to_all(sent, EVERYWHERE, split_axis=0, concat_axis=0, tiled=True)
    whole, back = steps(w, recv, modes)
    whole = lax.all_to_all(whole, EVERYWHERE, split_axis=0, concat_axis=0, tiled=True)
    back = lax.all_to_all(back, "narrow", split_axis=0, concat_axis=0, tiled=True)
    factor = gather_gram(whole)
    state = owner(back)[:, None]
    return (state, factor)


def solution(mesh):
    placed = (P(None, "wide", "narrow", None), P(None, None, "wide", "narrow"))
    return jax.shard_map(
        local,
        mesh=mesh,
        in_specs=placed,
        out_specs=(P(None, "wide", "narrow", None), P()),
        check_vma=False,
    )
```

```python
import functools

import jax
import jax.numpy as jnp
from jax import lax
from jax.experimental import pallas as pl
from jax.experimental.pallas import tpu as pltpu
from jax.sharding import PartitionSpec as P

GAMMA = 1.4
TIME_STEP = 0.25
VISCOSITY = 0.15
HALO = 4
WIDE = 16
NARROW = 8
DEVICES = WIDE * NARROW
MODES = 124
COLS = 128
ZPART = 32
WINDOW = ZPART + 2 * HALO
YPART = 8
NY = 64
INVERSE_CELLS = 1.0 / 262144.0
EVERYWHERE = ("wide", "narrow")
F32 = jnp.float32
BF16 = jnp.bfloat16


def lanes(shape):
    return lax.broadcasted_iota(jnp.int32, shape, len(shape) - 1)


def pack_kernel(fields_hbm, modes_hbm, out_hbm, modes_ref, known_ref, fields_ref, out_ref, sem):
    copies = [
        pltpu.make_async_copy(modes_hbm.at[c], modes_ref.at[c], sem.at[c]) for c in range(5)
    ]
    own = pltpu.make_async_copy(fields_hbm, fields_ref, sem.at[5])
    own.start()
    for copy in copies:
        copy.start()
    own.wait()
    lane = lanes((YPART, 128))
    lane_full = lanes((COLS, 128))
    means = []
    shifted = []
    for c in range(5):
        field = fields_ref[c]
        total = jnp.sum(jnp.sum(field, axis=0, keepdims=True), axis=1, keepdims=True)
        mean = (total * (1.0 / (YPART * 256))).astype(BF16).astype(F32)
        rounded = (field - mean).astype(BF16).astype(F32)
        known_ref[c] = rounded + mean
        means.append(jnp.broadcast_to(mean, (YPART, 128)))
        shifted.append(rounded)
    tail = jnp.zeros((YPART, 128), F32)
    for c in range(5):
        tail = jnp.where(lane == 3 * WINDOW + c, means[c], tail)
    halves = []
    for n in range(NARROW):
        def window(c, place):
            amount = (place * WINDOW + HALO - ZPART * n) % 256
            moved = pltpu.roll(shifted[c], amount, 1) if amount else shifted[c]
            return moved[:, 0:128]

        first = jnp.where(
            lane < WINDOW,
            window(0, 0),
            jnp.where(lane < 2 * WINDOW, window(1, 1), window(2, 2)),
        )
        first = jnp.where(lane < 3 * WINDOW, first, tail)
        second = jnp.where(lane < WINDOW, window(3, 0), window(4, 1))
        halves.append((first, second))

    gram = jnp.zeros((MODES, MODES), F32)
    for c in range(5):
        copies[c].wait()
        block = modes_ref[c]
        gram += lax.dot_general(
            block, block, (((1,), (1,)), ((), ())), preferred_element_type=F32
        )
    gram = jnp.concatenate([gram, jnp.zeros((MODES, COLS - MODES), F32)], axis=1)
    gram = jnp.concatenate([gram, jnp.zeros((COLS - MODES, 128), F32)], axis=0)
    high = gram.astype(BF16).astype(F32)
    rest = gram - high
    middle = rest.astype(BF16).astype(F32)
    low = rest - middle
    sends = []
    for n in range(NARROW):
        def turned(x, place):
            amount = (place - 16 * n) % 128
            return pltpu.roll(x, amount, 1) if amount else x

        first, second = halves[n]
        parts = jnp.where(
            lane_full < 96,
            turned(high, 80),
            jnp.where(lane_full < 112, turned(middle, 96), turned(low, 112)),
        ).reshape(WIDE, YPART, 128)
        lower = jnp.broadcast_to(first[None], (WIDE, YPART, 128))
        upper = jnp.where(lane[None] < 2 * WINDOW, second[None], parts)
        out_ref[:, n] = jnp.concatenate([lower, upper], axis=1).astype(BF16)
        send = pltpu.make_async_copy(out_ref.at[:, n], out_hbm.at[:, n], sem.at[6 + n])
        send.start()
        sends.append(send)
    for send in sends:
        send.wait()


def pack(fields, modes):
    return pl.pallas_call(
        pack_kernel,
        in_specs=[
            pl.BlockSpec(memory_space=pltpu.HBM),
            pl.BlockSpec(memory_space=pltpu.HBM),
        ],
        out_specs=[
            pl.BlockSpec(memory_space=pltpu.HBM),
            pl.BlockSpec(memory_space=pltpu.VMEM),
            pl.BlockSpec(memory_space=pltpu.VMEM),
        ],
        out_shape=[
            pltpu.HBM((WIDE, NARROW, 16, 128), BF16),
            jax.ShapeDtypeStruct((5, MODES, 2048), BF16),
            jax.ShapeDtypeStruct((5, YPART, 256), F32),
        ],
        scratch_shapes=[
            pltpu.VMEM((5, YPART, 256), F32),
            pltpu.VMEM((WIDE, NARROW, 16, 128), BF16),
            pltpu.SemaphoreType.DMA((6 + NARROW,)),
        ],
        name="pack",
        compiler_params=pltpu.CompilerParams(vmem_limit_bytes=16 * 2**20),
    )(
        pltpu.with_memory_space_constraint(fields, pltpu.HBM),
        pltpu.with_memory_space_constraint(modes, pltpu.HBM),
    )


def up(x, axis):
    return pltpu.roll(x, x.shape[axis] - 1, axis)


def down(x, axis):
    return pltpu.roll(x, 1, axis)


def fluxes(u, directions):
    density, m1, m2, m3, energy = u
    half = 0.5 * TIME_STEP
    share = half / density
    momenta = (m1, m2, m3)
    v = [m * share for m in momenta]
    products = {(i, i): momenta[i] * v[i] for i in range(3)}
    squares = products[(0, 0)] + products[(1, 1)] + products[(2, 2)]
    pressure = (half * (GAMMA - 1.0)) * energy - (0.5 * (GAMMA - 1.0)) * squares
    total = energy + (1.0 / half) * pressure
    out = []
    for d in directions:
        row = [half * momenta[d]]
        for i in range(3):
            if i == d:
                row.append(products[(d, d)] + pressure)
            else:
                key = (min(i, d), max(i, d))
                if key not in products:
                    products[key] = momenta[key[0]] * v[key[1]]
                row.append(products[key])
        row.append(total * v[d])
        out.append(row)
    return out


CENTRE = 1.0 - 6.0 * VISCOSITY * TIME_STEP
SOFT = VISCOSITY * TIME_STEP


def across(u):
    flux = fluxes(u, (0,))[0]
    smooth = [SOFT * x for x in u]
    ahead = [smooth[c] - flux[c] for c in range(5)]
    behind = [smooth[c] + flux[c] for c in range(5)]
    return ahead, behind


def within(u):
    rows = fluxes(u, (0, 1, 2))
    smooth = [SOFT * x for x in u]
    ahead = [smooth[c] - rows[0][c] for c in range(5)]
    behind = [smooth[c] + rows[0][c] for c in range(5)]
    total = []
    for c in range(5):
        total.append(
            CENTRE * u[c]
            + (up(smooth[c] - rows[1][c], 0) + down(smooth[c] + rows[1][c], 0))
            + (up(smooth[c] - rows[2][c], 1) + down(smooth[c] + rows[2][c], 1))
        )
    return ahead, behind, total


def joined(total, ahead, behind, after, before, lane):
    out = []
    for c in range(5):
        plus = pltpu.roll(ahead[c], 128 - WINDOW, 1)
        if after is not None:
            plus = jnp.where(lane < 2 * WINDOW, plus, pltpu.roll(after[c], 2 * WINDOW, 1))
        minus = pltpu.roll(behind[c], WINDOW, 1)
        if before is not None:
            minus = jnp.where(lane < WINDOW, pltpu.roll(before[c], 128 - 2 * WINDOW, 1), minus)
        out.append(total[c] + (plus + minus))
    return out


def section_all(load, lane):
    parts = []
    for g in range(3):
        parts.append(within(load(g)))
        if g >= 1:
            ahead, behind, total = parts[g - 1]
            before = parts[g - 2][1] if g >= 2 else None
            yield g - 1, joined(total, ahead, behind, parts[g][0], before, lane)
    ahead, behind, total = parts[2]
    yield 2, joined(total, ahead, behind, None, parts[1][1], lane)


def step_kernel(w_ref, recv_ref, modes_ref, whole_ref, base, one, two, turn_ref):
    w = w_ref[0]
    lane = lanes((NY, 128))

    for g in range(3):
        planes = []
        places = []
        for j in range(3):
            start = lax.rem(w + (3 * g - 4 + j + WIDE), WIDE) * NARROW
            block = recv_ref[pl.ds(start, NARROW)].astype(F32)
            planes.append((block[:, 0:8].reshape(NY, 128), block[:, 8:16].reshape(NY, 128)))
            places.append((lane >= WINDOW * j) & (lane < WINDOW * (j + 1)))
        for c in range(5):
            moved = []
            for j in range(3):
                amount = WINDOW * (j - c % 3) % 128
                value = planes[j][c // 3]
                moved.append(pltpu.roll(value, amount, 1) if amount else value)
            value = jnp.where(places[0], moved[0], jnp.where(places[1], moved[1], moved[2]))
            at = 3 * WINDOW + c
            mean = [
                jnp.broadcast_to(planes[j][0][:, at : at + 1], (NY, 128)) for j in range(3)
            ]
            mean = jnp.where(places[0], mean[0], jnp.where(places[1], mean[1], mean[2]))
            base[g, c] = value + mean

    terms = recv_ref[:, 8:16, :].astype(F32)
    summed = jnp.sum(terms, axis=0)
    block = (pltpu.roll(summed, 16, 1) + pltpu.roll(summed, 32, 1)) + pltpu.roll(summed, 48, 1)

    packed = [jnp.zeros((NY, 128), F32) for _ in range(5)]

    def keep(index, u, out):
        for c in range(5):
            value = pltpu.roll(u[c], (ZPART * index - WINDOW - HALO) % 128, 1)
            inside = (lane >= ZPART * index) & (lane < ZPART * (index + 1))
            out[c] = jnp.where(inside, value, out[c])

    def stored(ref):
        return lambda g: [ref[g, c] for c in range(5)]

    for g, v in section_all(stored(base), lane):
        for c in range(5):
            one[g, c] = v[c]
        if g == 1:
            keep(0, v, packed)
    for g, v in section_all(stored(one), lane):
        new = [0.5 * (base[g, c] + v[c]) for c in range(5)]
        for c in range(5):
            two[g, c] = new[c]
        if g == 1:
            keep(1, new, packed)
    outer = [jnp.where(lane < WINDOW, two[2, c], two[0, c]) for c in range(5)]
    after, before = across(outer)
    ahead, behind, total = within([two[1, c] for c in range(5)])
    third = joined(total, ahead, behind, after, before, lane)
    keep(2, third, packed)
    ahead, behind, total = within(third)
    fourth = joined(total, ahead, behind, None, None, lane)
    fourth = [0.5 * (two[1, c] + fourth[c]) for c in range(5)]
    keep(3, fourth, packed)
    change = [fourth[c] - base[1, c] for c in range(5)]
    spread = jnp.zeros((NY, 128), F32)
    for c in range(4):
        value = pltpu.roll(change[c], (ZPART * c - WINDOW - HALO) % 128, 1)
        inside = (lane >= ZPART * c) & (lane < ZPART * (c + 1))
        spread = jnp.where(inside, value, spread)
    last = pltpu.roll(change[4], 128 - WINDOW - HALO, 1)

    cross = jnp.zeros((4, MODES), F32)
    square = jnp.zeros((4, 4), F32)
    contract = (((1,), (1,)), ((), ()))
    for c in range(5):
        rounded = packed[c].astype(BF16).astype(F32)
        pair = jnp.concatenate([rounded, pltpu.roll(rounded, 127, 1)], axis=0)
        turn_ref[c] = pair.T
    for c in range(5):
        chunks = [turn_ref[c, pl.ds(2 * k, 4, stride=ZPART), :] for k in range(16)]
        rows = jnp.concatenate(chunks, axis=1).astype(BF16)
        cross += lax.dot_general(rows, modes_ref[c], contract, preferred_element_type=F32)
        square += lax.dot_general(rows, rows, contract, preferred_element_type=F32)
    top = jnp.concatenate([cross, square], axis=1) * INVERSE_CELLS
    high = top.astype(BF16).astype(F32)
    first = jnp.concatenate([high, top - high], axis=0)
    lane8 = lanes((8, 128))
    block = block * INVERSE_CELLS
    high = block.astype(BF16).astype(F32)
    rest = block - high
    middle = rest.astype(BF16).astype(F32)
    addends = jnp.where(
        lane8 < 48,
        pltpu.roll(high, 32, 1),
        jnp.where(lane8 < 64, pltpu.roll(middle, 48, 1), pltpu.roll(rest - middle, 64, 1)),
    )
    for n in range(NARROW):
        rows = slice(YPART * n, YPART * (n + 1))
        third_rows = jnp.where(lane8 < ZPART, last[rows], jnp.where(lane8 < 80, addends, 0.0))
        piece = jnp.concatenate([first, spread[rows], third_rows], axis=0).astype(BF16)
        whole_ref[:, n] = jnp.broadcast_to(piece[None], (WIDE, 24, 128))


def steps(w, recv, modes):
    return pl.pallas_call(
        step_kernel,
        in_specs=[
            pl.BlockSpec(memory_space=pltpu.SMEM),
            pl.BlockSpec(memory_space=pltpu.VMEM),
            pl.BlockSpec(memory_space=pltpu.VMEM),
        ],
        out_specs=pl.BlockSpec(memory_space=pltpu.VMEM),
        out_shape=jax.ShapeDtypeStruct((WIDE, NARROW, 24, 128), BF16),
        scratch_shapes=[
            pltpu.VMEM((3, 5, NY, 128), F32),
            pltpu.VMEM((3, 5, NY, 128), F32),
            pltpu.VMEM((3, 5, NY, 128), F32),
            pltpu.VMEM((5, 128, 128), F32),
        ],
        name="steps",
        compiler_params=pltpu.CompilerParams(vmem_limit_bytes=24 * 2**20),
    )(w, recv, modes)


def along_lanes(x, j):
    return jnp.broadcast_to(x[:, j : j + 1], x.shape)


def along_rows(x, i):
    return jnp.broadcast_to(x[i : i + 1, :], x.shape)


def factor_rows(panels):
    panels = list(panels)
    lane = lanes((8, 128))
    row = lax.broadcasted_iota(jnp.int32, (8, 128), 0)
    count = len(panels)
    done = []
    for k in range(count):
        base = 8 * k
        later = range(k + 1, count)
        columns = [along_lanes(panels[k], base + j) for j in range(8)]
        rows = [along_rows(panels[k], i) for i in range(8)]
        below = {q: [along_lanes(panels[q], base + j) for j in range(8)] for q in later}
        scaled = []
        out = jnp.zeros((8, 128), F32)
        for i in range(8):
            pivot = along_rows(columns[i], i)
            inverse = 1.0 / pivot
            for j in range(i + 1, 8):
                weight = along_rows(columns[j], i) * inverse
                columns[j] = columns[j] - columns[i] * weight
                rows[j] = rows[j] - rows[i] * weight
                for q in later:
                    below[q][j] = below[q][j] - below[q][i] * weight
            scaled.append(rows[i] * inverse)
            out = jnp.where(row == i, rows[i] * lax.rsqrt(pivot), out)
        done.append(jnp.where(lane >= row + base, out, 0.0))
        for q in later:
            change = [below[q][i] * scaled[i] for i in range(8)]
            while len(change) > 1:
                change = [change[t] + change[t + 1] for t in range(0, len(change), 2)]
            panels[q] = panels[q] - change[0]
    return done


def finish_kernel(w_ref, whole_ref, known_ref, factor_ref, state_ref):
    sums = jnp.sum(whole_ref[:, 0:8, :].astype(F32), axis=0)
    cross = sums[0:4] + sums[4:8]
    lane8 = lanes((8, 128))
    source = lax.broadcasted_iota(jnp.int32, (COLS, 128), 0)
    target = lanes((COLS, 128))
    gram = jnp.zeros((COLS, 128), F32)
    every = whole_ref[...].reshape(WIDE, NARROW, 24, 128)[:, :, 16:24, :].astype(F32)
    for b in range(8):
        held = (source >= ZPART) & (source < ZPART + 48) & (target >= 16 * b)
        chosen = jnp.where(held & (target == 16 * b + source % 16), 1.0, 0.0).astype(BF16)
        rows = every[:, b].reshape(COLS, 128).astype(BF16)
        gram += jnp.dot(rows, chosen, preferred_element_type=F32)
    panels = [gram[8 * a : 8 * a + 8] for a in range(16)]
    panels[15] = jnp.concatenate([panels[15][0:4], cross], axis=0)
    turned = jnp.concatenate([panels[15]] * 16, axis=0).T
    for a in range(16):
        panels[a] = jnp.where(lane8 >= MODES, turned[8 * a : 8 * a + 8], panels[a])
    for a, rows in enumerate(factor_rows(panels)):
        factor_ref[8 * a : 8 * a + 8, :] = rows

    home = whole_ref[pl.ds(w_ref[0] * NARROW, NARROW), 8:24, :].astype(F32)
    lane = lanes((YPART, 256))
    for c in range(5):
        total = jnp.zeros((YPART, 256), F32)
        place = ZPART * (c % 4)
        row = 8 * (c // 4)
        for n in range(NARROW):
            part = home[n, row : row + 8, :]
            part = jnp.concatenate([part, part], axis=1)
            amount = (ZPART * n - place) % 256
            part = pltpu.roll(part, amount, 1) if amount else part
            inside = (lane >= ZPART * n) & (lane < ZPART * (n + 1))
            total = jnp.where(inside, part, total)
        state_ref[c] = known_ref[c] + total


def finish(w, whole, known):
    return pl.pallas_call(
        finish_kernel,
        in_specs=[
            pl.BlockSpec(memory_space=pltpu.SMEM),
            pl.BlockSpec(memory_space=pltpu.VMEM),
            pl.BlockSpec(memory_space=pltpu.VMEM),
        ],
        out_shape=[
            jax.ShapeDtypeStruct((COLS, 128), F32),
            jax.ShapeDtypeStruct((5, YPART, 256), F32),
        ],
        name="finish",
        compiler_params=pltpu.CompilerParams(vmem_limit_bytes=16 * 2**20),
    )(w, whole, known)


def local(fields, prior_modes):
    modes = jnp.transpose(prior_modes[:, :, 0, :], (1, 0, 2))
    w = lax.axis_index("wide").astype(jnp.int32).reshape(1)
    sent, modes, known = pack(fields[:, 0], modes)
    sent = sent.reshape(DEVICES, 16, 128)
    recv = lax.all_to_all(sent, EVERYWHERE, split_axis=0, concat_axis=0, tiled=True)
    whole = steps(w, recv, modes).reshape(DEVICES, 24, 128)
    whole = lax.all_to_all(whole, EVERYWHERE, split_axis=0, concat_axis=0, tiled=True)
    factor, state = finish(w, whole, known)
    return (state[:, None], factor)


def solution(mesh):
    placed = (P(None, "wide", "narrow", None), P(None, None, "wide", "narrow"))
    return jax.shard_map(
        local,
        mesh=mesh,
        in_specs=placed,
        out_specs=(P(None, "wide", "narrow", None), P()),
        check_vma=False,
    )
```

```python
import functools

import jax
import jax.numpy as jnp
from jax import lax
from jax.experimental import pallas as pl
from jax.experimental.pallas import tpu as pltpu
from jax.sharding import PartitionSpec as P

GAMMA = 1.4
TIME_STEP = 0.25
VISCOSITY = 0.15
HALO = 4
WIDE = 16
NARROW = 8
DEVICES = WIDE * NARROW
CHIPS = WIDE // 2
MODES = 124
COLS = 128
ZPART = 32
WINDOW = ZPART + 2 * HALO
YPART = 8
NY = 64
INVERSE_CELLS = 1.0 / 262144.0
EVERYWHERE = ("wide", "narrow")
F32 = jnp.float32
BF16 = jnp.bfloat16


def lanes(shape):
    return lax.broadcasted_iota(jnp.int32, shape, len(shape) - 1)


def pack_kernel(fields_hbm, modes_hbm, out_ref, modes_ref, known_ref, fields_ref, sem):
    copies = [
        pltpu.make_async_copy(modes_hbm.at[c], modes_ref.at[c], sem.at[c]) for c in range(5)
    ]
    own = pltpu.make_async_copy(fields_hbm, fields_ref, sem.at[5])
    own.start()
    for copy in copies:
        copy.start()
    own.wait()
    lane = lanes((YPART, 128))
    lane_full = lanes((COLS, 128))
    means = []
    shifted = []
    for c in range(5):
        field = fields_ref[c]
        total = jnp.sum(jnp.sum(field, axis=0, keepdims=True), axis=1, keepdims=True)
        mean = (total * (1.0 / (YPART * 256))).astype(BF16).astype(F32)
        rounded = (field - mean).astype(BF16).astype(F32)
        known_ref[c] = rounded + mean
        means.append(jnp.broadcast_to(mean, (YPART, 128)))
        shifted.append(rounded)
    tail = jnp.zeros((YPART, 128), F32)
    for c in range(5):
        tail = jnp.where(lane == 3 * WINDOW + c, means[c], tail)
    halves = []
    for n in range(NARROW):
        def window(c, place):
            amount = (place * WINDOW + HALO - ZPART * n) % 256
            moved = pltpu.roll(shifted[c], amount, 1) if amount else shifted[c]
            return moved[:, 0:128]

        first = jnp.where(
            lane < WINDOW,
            window(0, 0),
            jnp.where(lane < 2 * WINDOW, window(1, 1), window(2, 2)),
        )
        first = jnp.where(lane < 3 * WINDOW, first, tail)
        second = jnp.where(lane < WINDOW, window(3, 0), window(4, 1))
        halves.append((first, second))

    gram = jnp.zeros((MODES, MODES), F32)
    for c in range(5):
        copies[c].wait()
        block = modes_ref[c]
        gram += lax.dot_general(
            block, block, (((1,), (1,)), ((), ())), preferred_element_type=F32
        )
    gram = jnp.concatenate([gram, jnp.zeros((MODES, COLS - MODES), F32)], axis=1)
    gram = jnp.concatenate([gram, jnp.zeros((COLS - MODES, 128), F32)], axis=0)
    high = gram.astype(BF16).astype(F32)
    rest = gram - high
    middle = rest.astype(BF16).astype(F32)
    low = rest - middle
    for n in range(NARROW):
        def turned(x, place):
            amount = (place - 16 * n) % 128
            return pltpu.roll(x, amount, 1) if amount else x

        first, second = halves[n]
        parts = jnp.where(
            lane_full < 96,
            turned(high, 80),
            jnp.where(lane_full < 112, turned(middle, 96), turned(low, 112)),
        ).reshape(WIDE, YPART, 128)
        lower = jnp.broadcast_to(first[None], (WIDE, YPART, 128))
        upper = jnp.where(lane[None] < 2 * WINDOW, second[None], parts)
        out_ref[:, n] = jnp.concatenate([lower, upper], axis=1).astype(BF16)


def pack(fields, modes):
    return pl.pallas_call(
        pack_kernel,
        in_specs=[
            pl.BlockSpec(memory_space=pltpu.HBM),
            pl.BlockSpec(memory_space=pltpu.HBM),
        ],
        out_specs=[
            pl.BlockSpec(memory_space=pltpu.VMEM),
            pl.BlockSpec(memory_space=pltpu.VMEM),
            pl.BlockSpec(memory_space=pltpu.VMEM),
        ],
        out_shape=[
            jax.ShapeDtypeStruct((WIDE, NARROW, 16, 128), BF16),
            jax.ShapeDtypeStruct((5, MODES, 2048), BF16),
            jax.ShapeDtypeStruct((5, YPART, 256), F32),
        ],
        scratch_shapes=[
            pltpu.VMEM((5, YPART, 256), F32),
            pltpu.SemaphoreType.DMA((6,)),
        ],
        name="pack",
        compiler_params=pltpu.CompilerParams(vmem_limit_bytes=16 * 2**20),
    )(
        pltpu.with_memory_space_constraint(fields, pltpu.HBM),
        pltpu.with_memory_space_constraint(modes, pltpu.HBM),
    )


def up(x, axis):
    return pltpu.roll(x, x.shape[axis] - 1, axis)


def down(x, axis):
    return pltpu.roll(x, 1, axis)


def fluxes(u, directions):
    density, m1, m2, m3, energy = u
    half = 0.5 * TIME_STEP
    share = half / density
    momenta = (m1, m2, m3)
    v = [m * share for m in momenta]
    products = {(i, i): momenta[i] * v[i] for i in range(3)}
    squares = products[(0, 0)] + products[(1, 1)] + products[(2, 2)]
    pressure = (half * (GAMMA - 1.0)) * energy - (0.5 * (GAMMA - 1.0)) * squares
    total = energy + (1.0 / half) * pressure
    out = []
    for d in directions:
        row = [half * momenta[d]]
        for i in range(3):
            if i == d:
                row.append(products[(d, d)] + pressure)
            else:
                key = (min(i, d), max(i, d))
                if key not in products:
                    products[key] = momenta[key[0]] * v[key[1]]
                row.append(products[key])
        row.append(total * v[d])
        out.append(row)
    return out


CENTRE = 1.0 - 6.0 * VISCOSITY * TIME_STEP
SOFT = VISCOSITY * TIME_STEP


def across(u):
    flux = fluxes(u, (0,))[0]
    smooth = [SOFT * x for x in u]
    ahead = [smooth[c] - flux[c] for c in range(5)]
    behind = [smooth[c] + flux[c] for c in range(5)]
    return ahead, behind


def beside(above, below, edge, slot):
    edge[0, slot, 8 : 8 + NY] = above
    edge[0, slot, 8 + NY : 9 + NY] = above[0:1]
    edge[1, slot, 8 : 8 + NY] = below
    edge[1, slot, 7:8] = below[NY - 1 : NY]
    return edge[0, slot, 9 : 9 + NY] + edge[1, slot, 7 : 7 + NY]


def within(u, edge, slot):
    rows = fluxes(u, (0, 1, 2))
    smooth = [SOFT * x for x in u]
    ahead = [smooth[c] - rows[0][c] for c in range(5)]
    behind = [smooth[c] + rows[0][c] for c in range(5)]
    total = []
    for c in range(5):
        total.append(
            CENTRE * u[c]
            + beside(smooth[c] - rows[1][c], smooth[c] + rows[1][c], edge, 5 * slot + c)
            + (up(smooth[c] - rows[2][c], 1) + down(smooth[c] + rows[2][c], 1))
        )
    return ahead, behind, total


def joined(total, ahead, behind, after, before, lane):
    out = []
    for c in range(5):
        plus = pltpu.roll(ahead[c], 128 - WINDOW, 1)
        if after is not None:
            plus = jnp.where(lane < 2 * WINDOW, plus, pltpu.roll(after[c], 2 * WINDOW, 1))
        minus = pltpu.roll(behind[c], WINDOW, 1)
        if before is not None:
            minus = jnp.where(lane < WINDOW, pltpu.roll(before[c], 128 - 2 * WINDOW, 1), minus)
        out.append(total[c] + (plus + minus))
    return out


def section_all(load, lane, edge, slot):
    parts = []
    for g in range(3):
        parts.append(within(load(g), edge, slot + g))
        if g >= 1:
            ahead, behind, total = parts[g - 1]
            before = parts[g - 2][1] if g >= 2 else None
            yield g - 1, joined(total, ahead, behind, parts[g][0], before, lane)
    ahead, behind, total = parts[2]
    yield 2, joined(total, ahead, behind, None, parts[1][1], lane)


def step_kernel(w_ref, recv_ref, modes_ref, pair_ref, home_ref, base, one, two, turn_ref, edge):
    w = w_ref[0]
    lane = lanes((NY, 128))

    for g in range(3):
        planes = []
        places = []
        for j in range(3):
            start = lax.rem(w + (3 * g - 4 + j + WIDE), WIDE) * NARROW
            block = recv_ref[pl.ds(start, NARROW)].astype(F32)
            planes.append((block[:, 0:8].reshape(NY, 128), block[:, 8:16].reshape(NY, 128)))
            places.append((lane >= WINDOW * j) & (lane < WINDOW * (j + 1)))
        for c in range(5):
            moved = []
            for j in range(3):
                amount = WINDOW * (j - c % 3) % 128
                value = planes[j][c // 3]
                moved.append(pltpu.roll(value, amount, 1) if amount else value)
            value = jnp.where(places[0], moved[0], jnp.where(places[1], moved[1], moved[2]))
            at = 3 * WINDOW + c
            mean = [
                jnp.broadcast_to(planes[j][0][:, at : at + 1], (NY, 128)) for j in range(3)
            ]
            mean = jnp.where(places[0], mean[0], jnp.where(places[1], mean[1], mean[2]))
            base[g, c] = value + mean

    terms = recv_ref[:, 8:16, :].astype(F32)
    summed = jnp.sum(terms, axis=0)
    block = (pltpu.roll(summed, 16, 1) + pltpu.roll(summed, 32, 1)) + pltpu.roll(summed, 48, 1)

    packed = [jnp.zeros((NY, 128), F32) for _ in range(5)]

    def keep(index, u, out):
        for c in range(5):
            value = pltpu.roll(u[c], (ZPART * index - WINDOW - HALO) % 128, 1)
            inside = (lane >= ZPART * index) & (lane < ZPART * (index + 1))
            out[c] = jnp.where(inside, value, out[c])

    def stored(ref):
        return lambda g: [ref[g, c] for c in range(5)]

    for g, v in section_all(stored(base), lane, edge, 0):
        for c in range(5):
            one[g, c] = v[c]
        if g == 1:
            keep(0, v, packed)
    for g, v in section_all(stored(one), lane, edge, 3):
        new = [0.5 * (base[g, c] + v[c]) for c in range(5)]
        for c in range(5):
            two[g, c] = new[c]
        if g == 1:
            keep(1, new, packed)
    outer = [jnp.where(lane < WINDOW, two[2, c], two[0, c]) for c in range(5)]
    after, before = across(outer)
    ahead, behind, total = within([two[1, c] for c in range(5)], edge, 6)
    third = joined(total, ahead, behind, after, before, lane)
    keep(2, third, packed)
    ahead, behind, total = within(third, edge, 7)
    fourth = joined(total, ahead, behind, None, None, lane)
    fourth = [0.5 * (two[1, c] + fourth[c]) for c in range(5)]
    keep(3, fourth, packed)
    change = [fourth[c] - base[1, c] for c in range(5)]
    spread = jnp.zeros((NY, 128), F32)
    for c in range(4):
        value = pltpu.roll(change[c], (ZPART * c - WINDOW - HALO) % 128, 1)
        inside = (lane >= ZPART * c) & (lane < ZPART * (c + 1))
        spread = jnp.where(inside, value, spread)
    home_ref[0] = spread
    home_ref[1] = pltpu.roll(change[4], 128 - WINDOW - HALO, 1)

    cross = jnp.zeros((4, MODES), F32)
    square = jnp.zeros((4, 4), F32)
    contract = (((1,), (1,)), ((), ()))
    for c in range(5):
        rounded = packed[c].astype(BF16).astype(F32)
        pair = jnp.concatenate([rounded, pltpu.roll(rounded, 127, 1)], axis=0)
        turn_ref[c] = pair.T
    for c in range(5):
        chunks = [turn_ref[c, pl.ds(2 * k, 4, stride=ZPART), :] for k in range(16)]
        rows = jnp.concatenate(chunks, axis=1).astype(BF16)
        cross += lax.dot_general(rows, modes_ref[c], contract, preferred_element_type=F32)
        square += lax.dot_general(rows, rows, contract, preferred_element_type=F32)
    top = jnp.concatenate([cross, square], axis=1) * INVERSE_CELLS
    lane8 = lanes((8, 128))
    block = block * INVERSE_CELLS
    high = block.astype(BF16).astype(F32)
    rest = block - high
    middle = rest.astype(BF16).astype(F32)
    addends = jnp.where(
        lane8 < 48,
        pltpu.roll(high, 32, 1),
        jnp.where(lane8 < 64, pltpu.roll(middle, 48, 1), pltpu.roll(rest - middle, 64, 1)),
    )
    addends = jnp.where((lane8 >= ZPART) & (lane8 < 80), addends, 0.0)
    odd = lax.rem(w, 2) == 1
    pair_ref[0:4] = top
    pair_ref[4:8] = jnp.zeros((4, 128), F32)
    pair_ref[8:16] = jnp.where(odd, pltpu.roll(addends, 48, 1), addends)


def steps(w, recv, modes):
    return pl.pallas_call(
        step_kernel,
        in_specs=[
            pl.BlockSpec(memory_space=pltpu.SMEM),
            pl.BlockSpec(memory_space=pltpu.VMEM),
            pl.BlockSpec(memory_space=pltpu.VMEM),
        ],
        out_specs=[
            pl.BlockSpec(memory_space=pltpu.VMEM),
            pl.BlockSpec(memory_space=pltpu.VMEM),
        ],
        out_shape=[
            jax.ShapeDtypeStruct((16, 128), F32),
            jax.ShapeDtypeStruct((2, NY, 128), F32),
        ],
        scratch_shapes=[
            pltpu.VMEM((3, 5, NY, 128), F32),
            pltpu.VMEM((3, 5, NY, 128), F32),
            pltpu.VMEM((3, 5, NY, 128), F32),
            pltpu.VMEM((5, 128, 128), F32),
            pltpu.VMEM((2, 40, NY + 16, 128), F32),
        ],
        name="steps",
        compiler_params=pltpu.CompilerParams(vmem_limit_bytes=24 * 2**20),
    )(w, recv, modes)


def merge_kernel(pair_ref, other_ref, home_ref, whole_ref):
    both = pair_ref[...] + other_ref[...]
    top = both[0:4]
    high = top.astype(BF16).astype(F32)
    first = jnp.concatenate([high, top - high], axis=0)
    lane8 = lanes((8, 128))
    for n in range(NARROW):
        rows = slice(YPART * n, YPART * (n + 1))
        third = jnp.where(lane8 < ZPART, home_ref[1, rows], both[8:16])
        piece = jnp.concatenate([first, home_ref[0, rows], third], axis=0).astype(BF16)
        whole_ref[:, n] = jnp.broadcast_to(piece[None], (CHIPS, 24, 128))


def merge(pair, other, home):
    return pl.pallas_call(
        merge_kernel,
        in_specs=[pl.BlockSpec(memory_space=pltpu.VMEM)] * 3,
        out_specs=pl.BlockSpec(memory_space=pltpu.VMEM),
        out_shape=jax.ShapeDtypeStruct((CHIPS, NARROW, 24, 128), BF16),
        name="merge",
        compiler_params=pltpu.CompilerParams(vmem_limit_bytes=16 * 2**20),
    )(pair, other, home)


def along_lanes(x, j):
    return jnp.broadcast_to(x[:, j : j + 1], x.shape)


def along_rows(x, i):
    return jnp.broadcast_to(x[i : i + 1, :], x.shape)


def factor_rows(panels):
    panels = list(panels)
    lane = lanes((8, 128))
    row = lax.broadcasted_iota(jnp.int32, (8, 128), 0)
    count = len(panels)
    done = []
    for k in range(count):
        base = 8 * k
        later = range(k + 1, count)
        columns = [along_lanes(panels[k], base + j) for j in range(8)]
        rows = [along_rows(panels[k], i) for i in range(8)]
        below = {q: [along_lanes(panels[q], base + j) for j in range(8)] for q in later}
        scaled = []
        out = jnp.zeros((8, 128), F32)
        for i in range(8):
            pivot = along_rows(columns[i], i)
            inverse = 1.0 / pivot
            for j in range(i + 1, 8):
                weight = along_rows(columns[j], i) * inverse
                columns[j] = columns[j] - columns[i] * weight
                rows[j] = rows[j] - rows[i] * weight
                for q in later:
                    below[q][j] = below[q][j] - below[q][i] * weight
            scaled.append(rows[i] * inverse)
            out = jnp.where(row == i, rows[i] * lax.rsqrt(pivot), out)
        done.append(jnp.where(lane >= row + base, out, 0.0))
        for q in later:
            change = [below[q][i] * scaled[i] for i in range(8)]
            while len(change) > 1:
                change = [change[t] + change[t + 1] for t in range(0, len(change), 2)]
            panels[q] = panels[q] - change[0]
    return done


def finish_kernel(w_ref, whole_ref, known_ref, factor_ref, state_ref):
    sums = jnp.sum(whole_ref[:, 0:8, :].astype(F32), axis=0)
    cross = sums[0:4] + sums[4:8]
    lane8 = lanes((8, 128))
    source = lax.broadcasted_iota(jnp.int32, (COLS, 256), 0)
    target = lanes((COLS, 256))
    start = ZPART + 48 * (target // 128)
    gram = jnp.zeros((CHIPS * 8, 256), F32)
    every = whole_ref[...].reshape(CHIPS, NARROW, 24, 128)[:, :, 16:24, :].astype(F32)
    for b in range(8):
        held = (source >= start) & (source < start + 48)
        match = target % 128 == 16 * b + source % 16
        chosen = jnp.where(held & match, 1.0, 0.0).astype(BF16)
        rows = every[:, b].reshape(CHIPS * 8, 128).astype(BF16)
        gram += jnp.dot(rows, chosen, preferred_element_type=F32)
    panels = []
    for a in range(16):
        m, core = a // 2, a % 2
        panels.append(gram[8 * m : 8 * m + 8, 128 * core : 128 * core + 128])
    panels[15] = jnp.concatenate([panels[15][0:4], cross], axis=0)
    turned = jnp.concatenate([panels[15]] * 16, axis=0).T
    for a in range(16):
        panels[a] = jnp.where(lane8 >= MODES, turned[8 * a : 8 * a + 8], panels[a])
    for a, rows in enumerate(factor_rows(panels)):
        factor_ref[8 * a : 8 * a + 8, :] = rows

    home = whole_ref[pl.ds(lax.div(w_ref[0], 2) * NARROW, NARROW), 8:24, :].astype(F32)
    lane = lanes((YPART, 256))
    for c in range(5):
        total = jnp.zeros((YPART, 256), F32)
        place = ZPART * (c % 4)
        row = 8 * (c // 4)
        for n in range(NARROW):
            part = home[n, row : row + 8, :]
            part = jnp.concatenate([part, part], axis=1)
            amount = (ZPART * n - place) % 256
            part = pltpu.roll(part, amount, 1) if amount else part
            inside = (lane >= ZPART * n) & (lane < ZPART * (n + 1))
            total = jnp.where(inside, part, total)
        state_ref[c] = known_ref[c] + total


def finish(w, whole, known):
    return pl.pallas_call(
        finish_kernel,
        in_specs=[
            pl.BlockSpec(memory_space=pltpu.SMEM),
            pl.BlockSpec(memory_space=pltpu.VMEM),
            pl.BlockSpec(memory_space=pltpu.VMEM),
        ],
        out_shape=[
            jax.ShapeDtypeStruct((COLS, 128), F32),
            jax.ShapeDtypeStruct((5, YPART, 256), F32),
        ],
        name="finish",
        compiler_params=pltpu.CompilerParams(vmem_limit_bytes=16 * 2**20),
    )(w, whole, known)


def local(fields, prior_modes):
    modes = jnp.transpose(prior_modes[:, :, 0, :], (1, 0, 2))
    w = lax.axis_index("wide").astype(jnp.int32).reshape(1)
    sent, modes, known = pack(fields[:, 0], modes)
    sent, w = lax.optimization_barrier((sent.reshape(DEVICES, 16, 128), w))
    recv = lax.all_to_all(sent, EVERYWHERE, split_axis=0, concat_axis=0, tiled=True)
    pair, home = steps(w, recv, modes)
    other = lax.ppermute(pair, "wide", [(i, i ^ 1) for i in range(WIDE)])
    whole = merge(pair, other, home).reshape(CHIPS * NARROW, 24, 128)
    groups = [
        [(2 * m + core) * NARROW + n for m in range(CHIPS) for n in range(NARROW)]
        for core in range(2)
    ]
    whole = lax.all_to_all(
        whole, EVERYWHERE, split_axis=0, concat_axis=0, axis_index_groups=groups, tiled=True
    )
    factor, state = finish(w, whole, known)
    return (state[:, None], factor)


def solution(mesh):
    placed = (P(None, "wide", "narrow", None), P(None, None, "wide", "narrow"))
    return jax.shard_map(
        local,
        mesh=mesh,
        in_specs=placed,
        out_specs=(P(None, "wide", "narrow", None), P()),
        check_vma=False,
    )
```

```python
import functools

import jax
import jax.numpy as jnp
from jax import lax
from jax.experimental import pallas as pl
from jax.experimental.pallas import tpu as pltpu
from jax.sharding import PartitionSpec as P

GAMMA = 1.4
TIME_STEP = 0.25
VISCOSITY = 0.15
HALO = 4
WIDE = 16
NARROW = 8
DEVICES = WIDE * NARROW
CHIPS = WIDE // 2
MODES = 124
COLS = 128
ZPART = 32
WINDOW = ZPART + 2 * HALO
YPART = 8
NY = 64
INVERSE_CELLS = 1.0 / 262144.0
EVERYWHERE = ("wide", "narrow")
F32 = jnp.float32
BF16 = jnp.bfloat16


def lanes(shape):
    return lax.broadcasted_iota(jnp.int32, shape, len(shape) - 1)


def pack_kernel(fields_hbm, modes_hbm, out_ref, modes_ref, known_ref, fields_ref, sem):
    copies = [
        pltpu.make_async_copy(modes_hbm.at[c], modes_ref.at[c], sem.at[c]) for c in range(5)
    ]
    own = pltpu.make_async_copy(fields_hbm, fields_ref, sem.at[5])
    own.start()
    for copy in copies:
        copy.start()
    own.wait()
    lane = lanes((YPART, 128))
    lane_full = lanes((COLS, 128))
    means = []
    shifted = []
    for c in range(5):
        field = fields_ref[c]
        total = jnp.sum(jnp.sum(field, axis=0, keepdims=True), axis=1, keepdims=True)
        mean = (total * (1.0 / (YPART * 256))).astype(BF16).astype(F32)
        rounded = (field - mean).astype(BF16).astype(F32)
        known_ref[c] = rounded + mean
        means.append(jnp.broadcast_to(mean, (YPART, 128)))
        shifted.append(rounded)
    tail = jnp.zeros((YPART, 128), F32)
    for c in range(5):
        tail = jnp.where(lane == 3 * WINDOW + c, means[c], tail)
    halves = []
    for n in range(NARROW):
        def window(c, place):
            amount = (place * WINDOW + HALO - ZPART * n) % 256
            moved = pltpu.roll(shifted[c], amount, 1) if amount else shifted[c]
            return moved[:, 0:128]

        first = jnp.where(
            lane < WINDOW,
            window(0, 0),
            jnp.where(lane < 2 * WINDOW, window(1, 1), window(2, 2)),
        )
        first = jnp.where(lane < 3 * WINDOW, first, tail)
        second = jnp.where(lane < WINDOW, window(3, 0), window(4, 1))
        halves.append((first, second))

    gram = jnp.zeros((MODES, MODES), F32)
    for c in range(5):
        copies[c].wait()
        block = modes_ref[c]
        gram += lax.dot_general(
            block, block, (((1,), (1,)), ((), ())), preferred_element_type=F32
        )
    gram = jnp.concatenate([gram, jnp.zeros((MODES, COLS - MODES), F32)], axis=1)
    gram = jnp.concatenate([gram, jnp.zeros((COLS - MODES, 128), F32)], axis=0)
    high = gram.astype(BF16).astype(F32)
    rest = gram - high
    middle = rest.astype(BF16).astype(F32)
    low = rest - middle
    for n in range(NARROW):
        def turned(x, place):
            amount = (place - 16 * n) % 128
            return pltpu.roll(x, amount, 1) if amount else x

        first, second = halves[n]
        parts = jnp.where(
            lane_full < 96,
            turned(high, 80),
            jnp.where(lane_full < 112, turned(middle, 96), turned(low, 112)),
        ).reshape(WIDE, YPART, 128)
        lower = jnp.broadcast_to(first[None], (WIDE, YPART, 128))
        upper = jnp.where(lane[None] < 2 * WINDOW, second[None], parts)
        out_ref[:, n] = jnp.concatenate([lower, upper], axis=1).astype(BF16)


def pack(fields, modes):
    return pl.pallas_call(
        pack_kernel,
        in_specs=[
            pl.BlockSpec(memory_space=pltpu.HBM),
            pl.BlockSpec(memory_space=pltpu.HBM),
        ],
        out_specs=[
            pl.BlockSpec(memory_space=pltpu.VMEM),
            pl.BlockSpec(memory_space=pltpu.VMEM),
            pl.BlockSpec(memory_space=pltpu.VMEM),
        ],
        out_shape=[
            jax.ShapeDtypeStruct((WIDE, NARROW, 16, 128), BF16),
            jax.ShapeDtypeStruct((5, MODES, 2048), BF16),
            jax.ShapeDtypeStruct((5, YPART, 256), F32),
        ],
        scratch_shapes=[
            pltpu.VMEM((5, YPART, 256), F32),
            pltpu.SemaphoreType.DMA((6,)),
        ],
        name="pack",
        compiler_params=pltpu.CompilerParams(vmem_limit_bytes=16 * 2**20),
    )(
        pltpu.with_memory_space_constraint(fields, pltpu.HBM),
        pltpu.with_memory_space_constraint(modes, pltpu.HBM),
    )


def up(x, axis):
    return pltpu.roll(x, x.shape[axis] - 1, axis)


def down(x, axis):
    return pltpu.roll(x, 1, axis)


def fluxes(u, directions):
    density, m1, m2, m3, energy = u
    half = 0.5 * TIME_STEP
    share = half / density
    momenta = (m1, m2, m3)
    v = [m * share for m in momenta]
    products = {(i, i): momenta[i] * v[i] for i in range(3)}
    squares = products[(0, 0)] + products[(1, 1)] + products[(2, 2)]
    pressure = (half * (GAMMA - 1.0)) * energy - (0.5 * (GAMMA - 1.0)) * squares
    total = energy + (1.0 / half) * pressure
    out = []
    for d in directions:
        row = [half * momenta[d]]
        for i in range(3):
            if i == d:
                row.append(products[(d, d)] + pressure)
            else:
                key = (min(i, d), max(i, d))
                if key not in products:
                    products[key] = momenta[key[0]] * v[key[1]]
                row.append(products[key])
        row.append(total * v[d])
        out.append(row)
    return out


CENTRE = 1.0 - 6.0 * VISCOSITY * TIME_STEP
SOFT = VISCOSITY * TIME_STEP


def across(u):
    flux = fluxes(u, (0,))[0]
    smooth = [SOFT * x for x in u]
    ahead = [smooth[c] - flux[c] for c in range(5)]
    behind = [smooth[c] + flux[c] for c in range(5)]
    return ahead, behind


def beside(above, below, edge, slot):
    edge[0, slot, 8 : 8 + NY] = above
    edge[0, slot, 8 + NY : 9 + NY] = above[0:1]
    edge[1, slot, 8 : 8 + NY] = below
    edge[1, slot, 7:8] = below[NY - 1 : NY]
    return edge[0, slot, 9 : 9 + NY] + edge[1, slot, 7 : 7 + NY]


def within(u, edge, slot):
    rows = fluxes(u, (0, 1, 2))
    smooth = [SOFT * x for x in u]
    ahead = [smooth[c] - rows[0][c] for c in range(5)]
    behind = [smooth[c] + rows[0][c] for c in range(5)]
    total = []
    for c in range(5):
        total.append(
            CENTRE * u[c]
            + beside(smooth[c] - rows[1][c], smooth[c] + rows[1][c], edge, 5 * slot + c)
            + (up(smooth[c] - rows[2][c], 1) + down(smooth[c] + rows[2][c], 1))
        )
    return ahead, behind, total


def joined(total, ahead, behind, after, before, lane):
    out = []
    for c in range(5):
        plus = pltpu.roll(ahead[c], 128 - WINDOW, 1)
        if after is not None:
            plus = jnp.where(lane < 2 * WINDOW, plus, pltpu.roll(after[c], 2 * WINDOW, 1))
        minus = pltpu.roll(behind[c], WINDOW, 1)
        if before is not None:
            minus = jnp.where(lane < WINDOW, pltpu.roll(before[c], 128 - 2 * WINDOW, 1), minus)
        out.append(total[c] + (plus + minus))
    return out


def section_all(load, lane, edge, slot):
    parts = []
    for g in range(3):
        parts.append(within(load(g), edge, slot + g))
        if g >= 1:
            ahead, behind, total = parts[g - 1]
            before = parts[g - 2][1] if g >= 2 else None
            yield g - 1, joined(total, ahead, behind, parts[g][0], before, lane)
    ahead, behind, total = parts[2]
    yield 2, joined(total, ahead, behind, None, parts[1][1], lane)


def step_kernel(w_ref, recv_ref, modes_ref, pair_ref, home_ref, base, one, two, turn_ref, edge):
    w = w_ref[0]
    lane = lanes((NY, 128))

    for g in range(3):
        planes = []
        places = []
        for j in range(3):
            start = lax.rem(w + (3 * g - 4 + j + WIDE), WIDE) * NARROW
            block = recv_ref[pl.ds(start, NARROW)].astype(F32)
            planes.append((block[:, 0:8].reshape(NY, 128), block[:, 8:16].reshape(NY, 128)))
            places.append((lane >= WINDOW * j) & (lane < WINDOW * (j + 1)))
        for c in range(5):
            moved = []
            for j in range(3):
                amount = WINDOW * (j - c % 3) % 128
                value = planes[j][c // 3]
                moved.append(pltpu.roll(value, amount, 1) if amount else value)
            value = jnp.where(places[0], moved[0], jnp.where(places[1], moved[1], moved[2]))
            at = 3 * WINDOW + c
            mean = [
                jnp.broadcast_to(planes[j][0][:, at : at + 1], (NY, 128)) for j in range(3)
            ]
            mean = jnp.where(places[0], mean[0], jnp.where(places[1], mean[1], mean[2]))
            base[g, c] = value + mean

    terms = recv_ref[:, 8:16, :].astype(F32)
    summed = jnp.sum(terms, axis=0)
    block = (pltpu.roll(summed, 16, 1) + pltpu.roll(summed, 32, 1)) + pltpu.roll(summed, 48, 1)

    packed = [jnp.zeros((NY, 128), F32) for _ in range(5)]

    def keep(index, u, out):
        for c in range(5):
            value = pltpu.roll(u[c], (ZPART * index - WINDOW - HALO) % 128, 1)
            inside = (lane >= ZPART * index) & (lane < ZPART * (index + 1))
            out[c] = jnp.where(inside, value, out[c])

    def stored(ref):
        return lambda g: [ref[g, c] for c in range(5)]

    for g, v in section_all(stored(base), lane, edge, 0):
        for c in range(5):
            one[g, c] = v[c]
        if g == 1:
            keep(0, v, packed)
    for g, v in section_all(stored(one), lane, edge, 3):
        new = [0.5 * (base[g, c] + v[c]) for c in range(5)]
        for c in range(5):
            two[g, c] = new[c]
        if g == 1:
            keep(1, new, packed)
    outer = [jnp.where(lane < WINDOW, two[2, c], two[0, c]) for c in range(5)]
    after, before = across(outer)
    ahead, behind, total = within([two[1, c] for c in range(5)], edge, 6)
    third = joined(total, ahead, behind, after, before, lane)
    keep(2, third, packed)
    ahead, behind, total = within(third, edge, 7)
    fourth = joined(total, ahead, behind, None, None, lane)
    fourth = [0.5 * (two[1, c] + fourth[c]) for c in range(5)]
    keep(3, fourth, packed)
    change = [fourth[c] - base[1, c] for c in range(5)]
    spread = jnp.zeros((NY, 128), F32)
    for c in range(4):
        value = pltpu.roll(change[c], (ZPART * c - WINDOW - HALO) % 128, 1)
        inside = (lane >= ZPART * c) & (lane < ZPART * (c + 1))
        spread = jnp.where(inside, value, spread)
    home_ref[0] = spread
    home_ref[1] = pltpu.roll(change[4], 128 - WINDOW - HALO, 1)

    contract = (((1,), (1,)), ((), ()))
    for c in range(5):
        rounded = packed[c].astype(BF16).astype(F32)
        pair = jnp.concatenate([rounded, pltpu.roll(rounded, 127, 1)], axis=0)
        turn_ref[c] = pair.astype(BF16).T.astype(F32)
    chunks = [turn_ref[c, pl.ds(2 * k, 4, stride=ZPART), :] for c in range(5) for k in range(16)]
    rows = jnp.concatenate(chunks, axis=1).astype(BF16)
    every = jnp.concatenate([modes_ref[c] for c in range(5)], axis=1)
    cross = lax.dot_general(rows, every, contract, preferred_element_type=F32)
    square = lax.dot_general(rows, rows, contract, preferred_element_type=F32)
    top = jnp.concatenate([cross, square], axis=1) * INVERSE_CELLS
    lane8 = lanes((8, 128))
    block = block * INVERSE_CELLS
    high = block.astype(BF16).astype(F32)
    rest = block - high
    middle = rest.astype(BF16).astype(F32)
    addends = jnp.where(
        lane8 < 48,
        pltpu.roll(high, 32, 1),
        jnp.where(lane8 < 64, pltpu.roll(middle, 48, 1), pltpu.roll(rest - middle, 64, 1)),
    )
    addends = jnp.where((lane8 >= ZPART) & (lane8 < 80), addends, 0.0)
    odd = lax.rem(w, 2) == 1
    pair_ref[0:4] = top
    pair_ref[4:8] = jnp.zeros((4, 128), F32)
    pair_ref[8:16] = jnp.where(odd, pltpu.roll(addends, 48, 1), addends)


def steps(w, recv, modes):
    return pl.pallas_call(
        step_kernel,
        in_specs=[
            pl.BlockSpec(memory_space=pltpu.SMEM),
            pl.BlockSpec(memory_space=pltpu.VMEM),
            pl.BlockSpec(memory_space=pltpu.VMEM),
        ],
        out_specs=[
            pl.BlockSpec(memory_space=pltpu.VMEM),
            pl.BlockSpec(memory_space=pltpu.VMEM),
        ],
        out_shape=[
            jax.ShapeDtypeStruct((16, 128), F32),
            jax.ShapeDtypeStruct((2, NY, 128), F32),
        ],
        scratch_shapes=[
            pltpu.VMEM((3, 5, NY, 128), F32),
            pltpu.VMEM((3, 5, NY, 128), F32),
            pltpu.VMEM((3, 5, NY, 128), F32),
            pltpu.VMEM((5, 128, 128), F32),
            pltpu.VMEM((2, 40, NY + 16, 128), F32),
        ],
        name="steps",
        compiler_params=pltpu.CompilerParams(vmem_limit_bytes=24 * 2**20),
    )(w, recv, modes)


def merge_kernel(pair_ref, other_ref, home_ref, whole_ref):
    both = pair_ref[...] + other_ref[...]
    top = both[0:4]
    high = top.astype(BF16).astype(F32)
    first = jnp.concatenate([high, top - high], axis=0)
    lane8 = lanes((8, 128))
    for n in range(NARROW):
        rows = slice(YPART * n, YPART * (n + 1))
        third = jnp.where(lane8 < ZPART, home_ref[1, rows], both[8:16])
        piece = jnp.concatenate([first, home_ref[0, rows], third], axis=0).astype(BF16)
        whole_ref[:, n] = jnp.broadcast_to(piece[None], (CHIPS, 24, 128))


def merge(pair, other, home):
    return pl.pallas_call(
        merge_kernel,
        in_specs=[pl.BlockSpec(memory_space=pltpu.VMEM)] * 3,
        out_specs=pl.BlockSpec(memory_space=pltpu.VMEM),
        out_shape=jax.ShapeDtypeStruct((CHIPS, NARROW, 24, 128), BF16),
        name="merge",
        compiler_params=pltpu.CompilerParams(vmem_limit_bytes=16 * 2**20),
    )(pair, other, home)


def along_lanes(x, j):
    return jnp.broadcast_to(x[:, j : j + 1], x.shape)


def along_rows(x, i):
    return jnp.broadcast_to(x[i : i + 1, :], x.shape)


NEAR = 2


def tree(terms):
    terms = list(terms)
    while len(terms) > 1:
        terms = [
            terms[t] + terms[t + 1] if t + 1 < len(terms) else terms[t]
            for t in range(0, len(terms), 2)
        ]
    return terms[0]


def factor_rows(panels):
    panels = list(panels)
    lane = lanes((8, 128))
    row = lax.broadcasted_iota(jnp.int32, (8, 128), 0)
    count = len(panels)
    done = []
    for k in range(count):
        base = 8 * k
        near = range(k + 1, min(k + 1 + NEAR, count))
        far = range(k + 1 + NEAR, count)
        columns = [along_lanes(panels[k], base + j) for j in range(8)]
        rows = [along_rows(panels[k], i) for i in range(8)]
        below = {q: [along_lanes(panels[q], base + j) for j in range(8)] for q in near}
        scaled = []
        unit = []
        weights = {}
        for i in range(8):
            pivot = along_rows(columns[i], i)
            inverse = 1.0 / pivot
            for j in range(i + 1, 8):
                weight = along_rows(columns[j], i) * inverse
                weights[(i, j)] = weight
                columns[j] = columns[j] - columns[i] * weight
                rows[j] = rows[j] - rows[i] * weight
                for q in near:
                    below[q][j] = below[q][j] - below[q][i] * weight
            scaled.append(rows[i] * inverse)
            unit.append(rows[i] * lax.rsqrt(pivot))
        out = unit[7]
        for i in range(7):
            out = jnp.where(row == i, unit[i], out)
        done.append(jnp.where(lane >= row + base, out, 0.0))
        for q in near:
            panels[q] = panels[q] - tree(below[q][i] * scaled[i] for i in range(8))
        if len(far):
            answer = list(scaled)
            for i in range(6, -1, -1):
                answer[i] = scaled[i] - tree(
                    [weights[(i, j)] * answer[j] for j in range(7, i, -1)]
                )
            solved = answer[7]
            for i in range(7):
                solved = jnp.where(row == i, answer[i], solved)
            blank = jnp.zeros((8, 128), F32)
            factor = jnp.concatenate([blank] * k + [solved] + [blank] * (15 - k), axis=0)
            held = jnp.concatenate([panels[q] for q in far], axis=0)
            change = jnp.dot(
                held, factor, precision=lax.Precision.HIGHEST, preferred_element_type=F32
            )
            for t, q in enumerate(far):
                panels[q] = panels[q] - change[8 * t : 8 * t + 8]
    return done


def finish_kernel(w_ref, whole_ref, known_ref, factor_ref, state_ref):
    sums = jnp.sum(whole_ref[:, 0:8, :].astype(F32), axis=0)
    cross = sums[0:4] + sums[4:8]
    lane8 = lanes((8, 128))
    source = lax.broadcasted_iota(jnp.int32, (COLS, 256), 0)
    target = lanes((COLS, 256))
    start = ZPART + 48 * (target // 128)
    gram = jnp.zeros((CHIPS * 8, 256), F32)
    every = whole_ref[...].reshape(CHIPS, NARROW, 24, 128)[:, :, 16:24, :].astype(F32)
    for b in range(8):
        held = (source >= start) & (source < start + 48)
        match = target % 128 == 16 * b + source % 16
        chosen = jnp.where(held & match, 1.0, 0.0).astype(BF16)
        rows = every[:, b].reshape(CHIPS * 8, 128).astype(BF16)
        gram += jnp.dot(rows, chosen, preferred_element_type=F32)
    panels = []
    for a in range(16):
        m, core = a // 2, a % 2
        panels.append(gram[8 * m : 8 * m + 8, 128 * core : 128 * core + 128])
    panels[15] = jnp.concatenate([panels[15][0:4], cross], axis=0)
    turned = jnp.concatenate([panels[15]] * 16, axis=0).T
    for a in range(16):
        panels[a] = jnp.where(lane8 >= MODES, turned[8 * a : 8 * a + 8], panels[a])
    for a, rows in enumerate(factor_rows(panels)):
        factor_ref[8 * a : 8 * a + 8, :] = rows

    home = whole_ref[pl.ds(lax.div(w_ref[0], 2) * NARROW, NARROW), 8:24, :].astype(F32)
    lane = lanes((YPART, 256))
    for c in range(5):
        total = jnp.zeros((YPART, 256), F32)
        place = ZPART * (c % 4)
        row = 8 * (c // 4)
        for n in range(NARROW):
            part = home[n, row : row + 8, :]
            part = jnp.concatenate([part, part], axis=1)
            amount = (ZPART * n - place) % 256
            part = pltpu.roll(part, amount, 1) if amount else part
            inside = (lane >= ZPART * n) & (lane < ZPART * (n + 1))
            total = jnp.where(inside, part, total)
        state_ref[c] = known_ref[c] + total


def finish(w, whole, known):
    return pl.pallas_call(
        finish_kernel,
        in_specs=[
            pl.BlockSpec(memory_space=pltpu.SMEM),
            pl.BlockSpec(memory_space=pltpu.VMEM),
            pl.BlockSpec(memory_space=pltpu.VMEM),
        ],
        out_shape=[
            jax.ShapeDtypeStruct((COLS, 128), F32),
            jax.ShapeDtypeStruct((5, YPART, 256), F32),
        ],
        name="finish",
        compiler_params=pltpu.CompilerParams(vmem_limit_bytes=16 * 2**20),
    )(w, whole, known)


def local(fields, prior_modes):
    modes = jnp.transpose(prior_modes[:, :, 0, :], (1, 0, 2))
    w = lax.axis_index("wide").astype(jnp.int32).reshape(1)
    sent, modes, known = pack(fields[:, 0], modes)
    sent, w = lax.optimization_barrier((sent.reshape(DEVICES, 16, 128), w))
    recv = lax.all_to_all(sent, EVERYWHERE, split_axis=0, concat_axis=0, tiled=True)
    pair, home = steps(w, recv, modes)
    other = lax.ppermute(pair, "wide", [(i, i ^ 1) for i in range(WIDE)])
    whole = merge(pair, other, home).reshape(CHIPS * NARROW, 24, 128)
    groups = [
        [(2 * m + core) * NARROW + n for m in range(CHIPS) for n in range(NARROW)]
        for core in range(2)
    ]
    whole = lax.all_to_all(
        whole, EVERYWHERE, split_axis=0, concat_axis=0, axis_index_groups=groups, tiled=True
    )
    factor, state = finish(w, whole, known)
    return (state[:, None], factor)


def solution(mesh):
    placed = (P(None, "wide", "narrow", None), P(None, None, "wide", "narrow"))
    return jax.shard_map(
        local,
        mesh=mesh,
        in_specs=placed,
        out_specs=(P(None, "wide", "narrow", None), P()),
        check_vma=False,
    )
```

```python
import functools

import jax
import jax.numpy as jnp
from jax import lax
from jax.experimental import pallas as pl
from jax.experimental.pallas import tpu as pltpu
from jax.sharding import PartitionSpec as P

GAMMA = 1.4
TIME_STEP = 0.25
VISCOSITY = 0.15
HALO = 4
WIDE = 16
NARROW = 8
DEVICES = WIDE * NARROW
CHIPS = WIDE // 2
MODES = 124
COLS = 128
ZPART = 32
WINDOW = ZPART + 2 * HALO
YPART = 8
NY = 64
INVERSE_CELLS = 1.0 / 262144.0
EVERYWHERE = ("wide", "narrow")
F32 = jnp.float32
BF16 = jnp.bfloat16


def lanes(shape):
    return lax.broadcasted_iota(jnp.int32, shape, len(shape) - 1)


def pack_kernel(fields_hbm, modes_hbm, out_ref, modes_ref, known_ref, fields_ref, sem):
    copies = [
        pltpu.make_async_copy(modes_hbm.at[c], modes_ref.at[c], sem.at[c]) for c in range(5)
    ]
    own = pltpu.make_async_copy(fields_hbm, fields_ref, sem.at[5])
    own.start()
    for copy in copies:
        copy.start()
    own.wait()
    lane = lanes((YPART, 128))
    lane_full = lanes((COLS, 128))
    means = []
    shifted = []
    for c in range(5):
        field = fields_ref[c]
        total = jnp.sum(jnp.sum(field, axis=0, keepdims=True), axis=1, keepdims=True)
        mean = (total * (1.0 / (YPART * 256))).astype(BF16).astype(F32)
        rounded = (field - mean).astype(BF16).astype(F32)
        known_ref[c] = rounded + mean
        means.append(jnp.broadcast_to(mean, (YPART, 128)))
        shifted.append(rounded)
    tail = jnp.zeros((YPART, 128), F32)
    for c in range(5):
        tail = jnp.where(lane == 3 * WINDOW + c, means[c], tail)
    halves = []
    for n in range(NARROW):
        def window(c, place):
            amount = (place * WINDOW + HALO - ZPART * n) % 256
            moved = pltpu.roll(shifted[c], amount, 1) if amount else shifted[c]
            return moved[:, 0:128]

        first = jnp.where(
            lane < WINDOW,
            window(0, 0),
            jnp.where(lane < 2 * WINDOW, window(1, 1), window(2, 2)),
        )
        first = jnp.where(lane < 3 * WINDOW, first, tail)
        second = jnp.where(lane < WINDOW, window(3, 0), window(4, 1))
        halves.append((first, second))

    gram = jnp.zeros((MODES, MODES), F32)
    for c in range(5):
        copies[c].wait()
        block = modes_ref[c]
        gram += lax.dot_general(
            block, block, (((1,), (1,)), ((), ())), preferred_element_type=F32
        )
    gram = jnp.concatenate([gram, jnp.zeros((MODES, COLS - MODES), F32)], axis=1)
    gram = jnp.concatenate([gram, jnp.zeros((COLS - MODES, 128), F32)], axis=0)
    high = gram.astype(BF16).astype(F32)
    rest = gram - high
    middle = rest.astype(BF16).astype(F32)
    low = rest - middle
    for n in range(NARROW):
        def turned(x, place):
            amount = (place - 16 * n) % 128
            return pltpu.roll(x, amount, 1) if amount else x

        first, second = halves[n]
        parts = jnp.where(
            lane_full < 96,
            turned(high, 80),
            jnp.where(lane_full < 112, turned(middle, 96), turned(low, 112)),
        ).reshape(WIDE, YPART, 128)
        lower = jnp.broadcast_to(first[None], (WIDE, YPART, 128))
        upper = jnp.where(lane[None] < 2 * WINDOW, second[None], parts)
        out_ref[:, n] = jnp.concatenate([lower, upper], axis=1).astype(BF16)


def pack(fields, modes):
    return pl.pallas_call(
        pack_kernel,
        in_specs=[
            pl.BlockSpec(memory_space=pltpu.HBM),
            pl.BlockSpec(memory_space=pltpu.HBM),
        ],
        out_specs=[
            pl.BlockSpec(memory_space=pltpu.VMEM),
            pl.BlockSpec(memory_space=pltpu.VMEM),
            pl.BlockSpec(memory_space=pltpu.VMEM),
        ],
        out_shape=[
            jax.ShapeDtypeStruct((WIDE, NARROW, 16, 128), BF16),
            jax.ShapeDtypeStruct((5, MODES, 2048), BF16),
            jax.ShapeDtypeStruct((5, YPART, 256), F32),
        ],
        scratch_shapes=[
            pltpu.VMEM((5, YPART, 256), F32),
            pltpu.SemaphoreType.DMA((6,)),
        ],
        name="pack",
        compiler_params=pltpu.CompilerParams(vmem_limit_bytes=16 * 2**20),
    )(
        pltpu.with_memory_space_constraint(fields, pltpu.HBM),
        pltpu.with_memory_space_constraint(modes, pltpu.HBM),
    )


def up(x, axis):
    return pltpu.roll(x, x.shape[axis] - 1, axis)


def down(x, axis):
    return pltpu.roll(x, 1, axis)


def fluxes(u, directions):
    density, m1, m2, m3, energy = u
    half = 0.5 * TIME_STEP
    share = half / density
    momenta = (m1, m2, m3)
    v = [m * share for m in momenta]
    products = {(i, i): momenta[i] * v[i] for i in range(3)}
    squares = products[(0, 0)] + products[(1, 1)] + products[(2, 2)]
    pressure = (half * (GAMMA - 1.0)) * energy - (0.5 * (GAMMA - 1.0)) * squares
    total = energy + (1.0 / half) * pressure
    out = []
    for d in directions:
        row = [half * momenta[d]]
        for i in range(3):
            if i == d:
                row.append(products[(d, d)] + pressure)
            else:
                key = (min(i, d), max(i, d))
                if key not in products:
                    products[key] = momenta[key[0]] * v[key[1]]
                row.append(products[key])
        row.append(total * v[d])
        out.append(row)
    return out


CENTRE = 1.0 - 6.0 * VISCOSITY * TIME_STEP
SOFT = VISCOSITY * TIME_STEP


def across(u):
    flux = fluxes(u, (0,))[0]
    smooth = [SOFT * x for x in u]
    ahead = [smooth[c] - flux[c] for c in range(5)]
    behind = [smooth[c] + flux[c] for c in range(5)]
    return ahead, behind


def beside(above, below, edge, slot):
    edge[0, slot, 8 : 8 + NY] = above
    edge[0, slot, 8 + NY : 9 + NY] = above[0:1]
    edge[1, slot, 8 : 8 + NY] = below
    edge[1, slot, 7:8] = below[NY - 1 : NY]
    return edge[0, slot, 9 : 9 + NY] + edge[1, slot, 7 : 7 + NY]


def within(u, edge, slot):
    rows = fluxes(u, (0, 1, 2))
    smooth = [SOFT * x for x in u]
    ahead = [smooth[c] - rows[0][c] for c in range(5)]
    behind = [smooth[c] + rows[0][c] for c in range(5)]
    total = []
    for c in range(5):
        total.append(
            CENTRE * u[c]
            + beside(smooth[c] - rows[1][c], smooth[c] + rows[1][c], edge, 5 * slot + c)
            + (up(smooth[c] - rows[2][c], 1) + down(smooth[c] + rows[2][c], 1))
        )
    return ahead, behind, total


def joined(total, ahead, behind, after, before, lane):
    out = []
    for c in range(5):
        plus = pltpu.roll(ahead[c], 128 - WINDOW, 1)
        if after is not None:
            plus = jnp.where(lane < 2 * WINDOW, plus, pltpu.roll(after[c], 2 * WINDOW, 1))
        minus = pltpu.roll(behind[c], WINDOW, 1)
        if before is not None:
            minus = jnp.where(lane < WINDOW, pltpu.roll(before[c], 128 - 2 * WINDOW, 1), minus)
        out.append(total[c] + (plus + minus))
    return out


def section_all(load, lane, edge, slot):
    parts = []
    for g in range(3):
        parts.append(within(load(g), edge, slot + g))
        if g >= 1:
            ahead, behind, total = parts[g - 1]
            before = parts[g - 2][1] if g >= 2 else None
            yield g - 1, joined(total, ahead, behind, parts[g][0], before, lane)
    ahead, behind, total = parts[2]
    yield 2, joined(total, ahead, behind, None, parts[1][1], lane)


def step_kernel(w_ref, recv_ref, modes_ref, pair_ref, home_ref, base, one, two, turn_ref, edge):
    w = w_ref[0]
    lane = lanes((NY, 128))

    for g in range(3):
        planes = []
        places = []
        for j in range(3):
            start = lax.rem(w + (3 * g - 4 + j + WIDE), WIDE) * NARROW
            block = recv_ref[pl.ds(start, NARROW)].astype(F32)
            planes.append((block[:, 0:8].reshape(NY, 128), block[:, 8:16].reshape(NY, 128)))
            places.append((lane >= WINDOW * j) & (lane < WINDOW * (j + 1)))
        for c in range(5):
            moved = []
            for j in range(3):
                amount = WINDOW * (j - c % 3) % 128
                value = planes[j][c // 3]
                moved.append(pltpu.roll(value, amount, 1) if amount else value)
            value = jnp.where(places[0], moved[0], jnp.where(places[1], moved[1], moved[2]))
            at = 3 * WINDOW + c
            mean = [
                jnp.broadcast_to(planes[j][0][:, at : at + 1], (NY, 128)) for j in range(3)
            ]
            mean = jnp.where(places[0], mean[0], jnp.where(places[1], mean[1], mean[2]))
            base[g, c] = value + mean

    terms = recv_ref[:, 8:16, :].astype(F32)
    summed = jnp.sum(terms, axis=0)
    block = (pltpu.roll(summed, 16, 1) + pltpu.roll(summed, 32, 1)) + pltpu.roll(summed, 48, 1)

    packed = [jnp.zeros((NY, 128), F32) for _ in range(5)]

    def keep(index, u, out):
        for c in range(5):
            value = pltpu.roll(u[c], (ZPART * index - WINDOW - HALO) % 128, 1)
            inside = (lane >= ZPART * index) & (lane < ZPART * (index + 1))
            out[c] = jnp.where(inside, value, out[c])

    def stored(ref):
        return lambda g: [ref[g, c] for c in range(5)]

    for g, v in section_all(stored(base), lane, edge, 0):
        for c in range(5):
            one[g, c] = v[c]
        if g == 1:
            keep(0, v, packed)
    first, middle, last = [stored(one)(g) for g in range(3)]
    side = [jnp.where(lane < WINDOW, last[c], first[c]) for c in range(5)]
    side_ahead, side_behind, side_total = within(side, edge, 3)
    ahead, behind, total = within(middle, edge, 4)
    far_ahead = across(last)[0]
    v = joined(total, ahead, behind, side_ahead, side_behind, lane)
    new = [0.5 * (base[1, c] + v[c]) for c in range(5)]
    for c in range(5):
        two[1, c] = new[c]
    keep(1, new, packed)
    outer = []
    for c in range(5):
        plus = jnp.where(
            lane < WINDOW,
            pltpu.roll(far_ahead[c], 128 - WINDOW, 1),
            pltpu.roll(ahead[c], 2 * WINDOW, 1),
        )
        minus = jnp.where(
            lane < WINDOW,
            pltpu.roll(behind[c], 128 - 2 * WINDOW, 1),
            pltpu.roll(side_behind[c], WINDOW, 1),
        )
        held = jnp.where(lane < WINDOW, base[2, c], base[0, c])
        outer.append(0.5 * (held + (side_total[c] + (plus + minus))))
    after, before = across(outer)
    ahead, behind, total = within([two[1, c] for c in range(5)], edge, 6)
    third = joined(total, ahead, behind, after, before, lane)
    keep(2, third, packed)
    ahead, behind, total = within(third, edge, 7)
    fourth = joined(total, ahead, behind, None, None, lane)
    fourth = [0.5 * (two[1, c] + fourth[c]) for c in range(5)]
    keep(3, fourth, packed)
    change = [fourth[c] - base[1, c] for c in range(5)]
    spread = jnp.zeros((NY, 128), F32)
    for c in range(4):
        value = pltpu.roll(change[c], (ZPART * c - WINDOW - HALO) % 128, 1)
        inside = (lane >= ZPART * c) & (lane < ZPART * (c + 1))
        spread = jnp.where(inside, value, spread)
    home_ref[0] = spread
    home_ref[1] = pltpu.roll(change[4], 128 - WINDOW - HALO, 1)

    contract = (((1,), (1,)), ((), ()))
    for c in range(5):
        rounded = packed[c].astype(BF16).astype(F32)
        pair = jnp.concatenate([rounded, pltpu.roll(rounded, 127, 1)], axis=0)
        turn_ref[c] = pair.astype(BF16).T.astype(F32)
    chunks = [turn_ref[c, pl.ds(2 * k, 4, stride=ZPART), :] for c in range(5) for k in range(16)]
    rows = jnp.concatenate(chunks, axis=1).astype(BF16)
    every = jnp.concatenate([modes_ref[c] for c in range(5)], axis=1)
    cross = lax.dot_general(rows, every, contract, preferred_element_type=F32)
    square = lax.dot_general(rows, rows, contract, preferred_element_type=F32)
    top = jnp.concatenate([cross, square], axis=1) * INVERSE_CELLS
    lane8 = lanes((8, 128))
    block = block * INVERSE_CELLS
    high = block.astype(BF16).astype(F32)
    rest = block - high
    middle = rest.astype(BF16).astype(F32)
    addends = jnp.where(
        lane8 < 48,
        pltpu.roll(high, 32, 1),
        jnp.where(lane8 < 64, pltpu.roll(middle, 48, 1), pltpu.roll(rest - middle, 64, 1)),
    )
    addends = jnp.where((lane8 >= ZPART) & (lane8 < 80), addends, 0.0)
    odd = lax.rem(w, 2) == 1
    pair_ref[0:4] = top
    pair_ref[4:8] = jnp.zeros((4, 128), F32)
    pair_ref[8:16] = jnp.where(odd, pltpu.roll(addends, 48, 1), addends)


def steps(w, recv, modes):
    return pl.pallas_call(
        step_kernel,
        in_specs=[
            pl.BlockSpec(memory_space=pltpu.SMEM),
            pl.BlockSpec(memory_space=pltpu.VMEM),
            pl.BlockSpec(memory_space=pltpu.VMEM),
        ],
        out_specs=[
            pl.BlockSpec(memory_space=pltpu.VMEM),
            pl.BlockSpec(memory_space=pltpu.VMEM),
        ],
        out_shape=[
            jax.ShapeDtypeStruct((16, 128), F32),
            jax.ShapeDtypeStruct((2, NY, 128), F32),
        ],
        scratch_shapes=[
            pltpu.VMEM((3, 5, NY, 128), F32),
            pltpu.VMEM((3, 5, NY, 128), F32),
            pltpu.VMEM((2, 5, NY, 128), F32),
            pltpu.VMEM((5, 128, 128), F32),
            pltpu.VMEM((2, 40, NY + 16, 128), F32),
        ],
        name="steps",
        compiler_params=pltpu.CompilerParams(vmem_limit_bytes=24 * 2**20),
    )(w, recv, modes)


def merge_kernel(pair_ref, other_ref, home_ref, whole_ref):
    both = pair_ref[...] + other_ref[...]
    top = both[0:4]
    high = top.astype(BF16).astype(F32)
    first = jnp.concatenate([high, top - high], axis=0)
    lane8 = lanes((8, 128))
    for n in range(NARROW):
        rows = slice(YPART * n, YPART * (n + 1))
        third = jnp.where(lane8 < ZPART, home_ref[1, rows], both[8:16])
        piece = jnp.concatenate([first, home_ref[0, rows], third], axis=0).astype(BF16)
        whole_ref[:, n] = jnp.broadcast_to(piece[None], (CHIPS, 24, 128))


def merge(pair, other, home):
    return pl.pallas_call(
        merge_kernel,
        in_specs=[pl.BlockSpec(memory_space=pltpu.VMEM)] * 3,
        out_specs=pl.BlockSpec(memory_space=pltpu.VMEM),
        out_shape=jax.ShapeDtypeStruct((CHIPS, NARROW, 24, 128), BF16),
        name="merge",
        compiler_params=pltpu.CompilerParams(vmem_limit_bytes=16 * 2**20),
    )(pair, other, home)


def along_lanes(x, j):
    return jnp.broadcast_to(x[:, j : j + 1], x.shape)


def along_rows(x, i):
    return jnp.broadcast_to(x[i : i + 1, :], x.shape)


NEAR = 2


def tree(terms):
    terms = list(terms)
    while len(terms) > 1:
        terms = [
            terms[t] + terms[t + 1] if t + 1 < len(terms) else terms[t]
            for t in range(0, len(terms), 2)
        ]
    return terms[0]


def factor_rows(panels):
    panels = list(panels)
    lane = lanes((8, 128))
    row = lax.broadcasted_iota(jnp.int32, (8, 128), 0)
    count = len(panels)
    done = []
    for k in range(count):
        base = 8 * k
        near = range(k + 1, min(k + 1 + NEAR, count))
        far = range(k + 1 + NEAR, count)
        columns = [along_lanes(panels[k], base + j) for j in range(8)]
        rows = [along_rows(panels[k], i) for i in range(8)]
        below = {q: [along_lanes(panels[q], base + j) for j in range(8)] for q in near}
        scaled = []
        unit = []
        weights = {}
        for i in range(8):
            pivot = along_rows(columns[i], i)
            inverse = 1.0 / pivot
            for j in range(i + 1, 8):
                weight = along_rows(columns[j], i) * inverse
                weights[(i, j)] = weight
                columns[j] = columns[j] - columns[i] * weight
                rows[j] = rows[j] - rows[i] * weight
                for q in near:
                    below[q][j] = below[q][j] - below[q][i] * weight
            scaled.append(rows[i] * inverse)
            unit.append(rows[i] * lax.rsqrt(pivot))
        out = unit[7]
        for i in range(7):
            out = jnp.where(row == i, unit[i], out)
        done.append(jnp.where(lane >= row + base, out, 0.0))
        for q in near:
            panels[q] = panels[q] - tree(below[q][i] * scaled[i] for i in range(8))
        if len(far):
            answer = list(scaled)
            for i in range(6, -1, -1):
                answer[i] = scaled[i] - tree(
                    [weights[(i, j)] * answer[j] for j in range(7, i, -1)]
                )
            solved = answer[7]
            for i in range(7):
                solved = jnp.where(row == i, answer[i], solved)
            blank = jnp.zeros((8, 128), F32)
            factor = jnp.concatenate([blank] * k + [solved] + [blank] * (15 - k), axis=0)
            held = jnp.concatenate([panels[q] for q in far], axis=0)
            change = jnp.dot(
                held, factor, precision=lax.Precision.HIGHEST, preferred_element_type=F32
            )
            for t, q in enumerate(far):
                panels[q] = panels[q] - change[8 * t : 8 * t + 8]
    return done


def finish_kernel(w_ref, whole_ref, known_ref, factor_ref, state_ref):
    sums = jnp.sum(whole_ref[:, 0:8, :].astype(F32), axis=0)
    cross = sums[0:4] + sums[4:8]
    lane8 = lanes((8, 128))
    source = lax.broadcasted_iota(jnp.int32, (COLS, 256), 0)
    target = lanes((COLS, 256))
    start = ZPART + 48 * (target // 128)
    gram = jnp.zeros((CHIPS * 8, 256), F32)
    every = whole_ref[...].reshape(CHIPS, NARROW, 24, 128)[:, :, 16:24, :].astype(F32)
    for b in range(8):
        held = (source >= start) & (source < start + 48)
        match = target % 128 == 16 * b + source % 16
        chosen = jnp.where(held & match, 1.0, 0.0).astype(BF16)
        rows = every[:, b].reshape(CHIPS * 8, 128).astype(BF16)
        gram += jnp.dot(rows, chosen, preferred_element_type=F32)
    panels = []
    for a in range(16):
        m, core = a // 2, a % 2
        panels.append(gram[8 * m : 8 * m + 8, 128 * core : 128 * core + 128])
    panels[15] = jnp.concatenate([panels[15][0:4], cross], axis=0)
    turned = jnp.concatenate([panels[15]] * 16, axis=0).T
    for a in range(16):
        panels[a] = jnp.where(lane8 >= MODES, turned[8 * a : 8 * a + 8], panels[a])
    for a, rows in enumerate(factor_rows(panels)):
        factor_ref[8 * a : 8 * a + 8, :] = rows

    home = whole_ref[pl.ds(lax.div(w_ref[0], 2) * NARROW, NARROW), 8:24, :].astype(F32)
    lane = lanes((YPART, 256))
    for c in range(5):
        total = jnp.zeros((YPART, 256), F32)
        place = ZPART * (c % 4)
        row = 8 * (c // 4)
        for n in range(NARROW):
            part = home[n, row : row + 8, :]
            part = jnp.concatenate([part, part], axis=1)
            amount = (ZPART * n - place) % 256
            part = pltpu.roll(part, amount, 1) if amount else part
            inside = (lane >= ZPART * n) & (lane < ZPART * (n + 1))
            total = jnp.where(inside, part, total)
        state_ref[c] = known_ref[c] + total


def finish(w, whole, known):
    return pl.pallas_call(
        finish_kernel,
        in_specs=[
            pl.BlockSpec(memory_space=pltpu.SMEM),
            pl.BlockSpec(memory_space=pltpu.VMEM),
            pl.BlockSpec(memory_space=pltpu.VMEM),
        ],
        out_shape=[
            jax.ShapeDtypeStruct((COLS, 128), F32),
            jax.ShapeDtypeStruct((5, YPART, 256), F32),
        ],
        name="finish",
        compiler_params=pltpu.CompilerParams(vmem_limit_bytes=16 * 2**20),
    )(w, whole, known)


def local(fields, prior_modes):
    modes = jnp.transpose(prior_modes[:, :, 0, :], (1, 0, 2))
    w = lax.axis_index("wide").astype(jnp.int32).reshape(1)
    sent, modes, known = pack(fields[:, 0], modes)
    sent, w = lax.optimization_barrier((sent.reshape(DEVICES, 16, 128), w))
    recv = lax.all_to_all(sent, EVERYWHERE, split_axis=0, concat_axis=0, tiled=True)
    pair, home = steps(w, recv, modes)
    other = lax.ppermute(pair, "wide", [(i, i ^ 1) for i in range(WIDE)])
    whole = merge(pair, other, home).reshape(CHIPS * NARROW, 24, 128)
    groups = [
        [(2 * m + core) * NARROW + n for m in range(CHIPS) for n in range(NARROW)]
        for core in range(2)
    ]
    whole = lax.all_to_all(
        whole, EVERYWHERE, split_axis=0, concat_axis=0, axis_index_groups=groups, tiled=True
    )
    factor, state = finish(w, whole, known)
    return (state[:, None], factor)


def solution(mesh):
    placed = (P(None, "wide", "narrow", None), P(None, None, "wide", "narrow"))
    return jax.shard_map(
        local,
        mesh=mesh,
        in_specs=placed,
        out_specs=(P(None, "wide", "narrow", None), P()),
        check_vma=False,
    )
```

```python
import functools

import jax
import jax.numpy as jnp
from jax import lax
from jax.experimental import pallas as pl
from jax.experimental.pallas import tpu as pltpu
from jax.sharding import PartitionSpec as P

GAMMA = 1.4
TIME_STEP = 0.25
VISCOSITY = 0.15
HALO = 4
WIDE = 16
NARROW = 8
DEVICES = WIDE * NARROW
CHIPS = WIDE // 2
MODES = 124
COLS = 128
ZPART = 32
WINDOW = ZPART + 2 * HALO
YPART = 8
NY = 64
INVERSE_CELLS = 1.0 / 262144.0
EVERYWHERE = ("wide", "narrow")
F32 = jnp.float32
BF16 = jnp.bfloat16


def lanes(shape):
    return lax.broadcasted_iota(jnp.int32, shape, len(shape) - 1)


def pack_kernel(fields_hbm, modes_hbm, out_ref, modes_ref, known_ref, fields_ref, sem):
    copies = [
        pltpu.make_async_copy(modes_hbm.at[c], modes_ref.at[c], sem.at[c]) for c in range(5)
    ]
    own = pltpu.make_async_copy(fields_hbm, fields_ref, sem.at[5])
    own.start()
    for copy in copies:
        copy.start()
    own.wait()
    lane = lanes((YPART, 128))
    lane_full = lanes((COLS, 128))
    means = []
    shifted = []
    for c in range(5):
        field = fields_ref[c]
        total = jnp.sum(jnp.sum(field, axis=0, keepdims=True), axis=1, keepdims=True)
        mean = (total * (1.0 / (YPART * 256))).astype(BF16).astype(F32)
        rounded = (field - mean).astype(BF16).astype(F32)
        known_ref[c] = rounded + mean
        means.append(jnp.broadcast_to(mean, (YPART, 128)))
        shifted.append(rounded)
    tail = jnp.zeros((YPART, 128), F32)
    for c in range(5):
        tail = jnp.where(lane == 3 * WINDOW + c, means[c], tail)
    halves = []
    for n in range(NARROW):
        def window(c, place):
            amount = (place * WINDOW + HALO - ZPART * n) % 256
            moved = pltpu.roll(shifted[c], amount, 1) if amount else shifted[c]
            return moved[:, 0:128]

        first = jnp.where(
            lane < WINDOW,
            window(0, 0),
            jnp.where(lane < 2 * WINDOW, window(1, 1), window(2, 2)),
        )
        first = jnp.where(lane < 3 * WINDOW, first, tail)
        second = jnp.where(lane < WINDOW, window(3, 0), window(4, 1))
        halves.append((first, second))

    gram = jnp.zeros((MODES, MODES), F32)
    for c in range(5):
        copies[c].wait()
        block = modes_ref[c]
        gram += lax.dot_general(
            block, block, (((1,), (1,)), ((), ())), preferred_element_type=F32
        )
    gram = jnp.concatenate([gram, jnp.zeros((MODES, COLS - MODES), F32)], axis=1)
    gram = jnp.concatenate([gram, jnp.zeros((COLS - MODES, 128), F32)], axis=0)
    high = gram.astype(BF16).astype(F32)
    rest = gram - high
    middle = rest.astype(BF16).astype(F32)
    low = rest - middle
    group = lax.div(lane_full, 16)
    middle_ahead = pltpu.roll(middle, 16, 1)
    low_ahead = pltpu.roll(low, 32, 1)
    for n in range(NARROW):
        first, second = halves[n]
        chosen = jnp.where(
            group == n, high, jnp.where(group == (n + 1) % 8, middle_ahead, low_ahead)
        )
        amount = (80 - 16 * n) % 128
        parts = (pltpu.roll(chosen, amount, 1) if amount else chosen).reshape(WIDE, YPART, 128)
        lower = jnp.broadcast_to(first[None], (WIDE, YPART, 128))
        upper = jnp.where(lane[None] < 2 * WINDOW, second[None], parts)
        out_ref[:, n] = jnp.concatenate([lower, upper], axis=1).astype(BF16)


def pack(fields, modes):
    return pl.pallas_call(
        pack_kernel,
        in_specs=[
            pl.BlockSpec(memory_space=pltpu.HBM),
            pl.BlockSpec(memory_space=pltpu.HBM),
        ],
        out_specs=[
            pl.BlockSpec(memory_space=pltpu.VMEM),
            pl.BlockSpec(memory_space=pltpu.VMEM),
            pl.BlockSpec(memory_space=pltpu.VMEM),
        ],
        out_shape=[
            jax.ShapeDtypeStruct((WIDE, NARROW, 16, 128), BF16),
            jax.ShapeDtypeStruct((5, MODES, 2048), BF16),
            jax.ShapeDtypeStruct((5, YPART, 256), F32),
        ],
        scratch_shapes=[
            pltpu.VMEM((5, YPART, 256), F32),
            pltpu.SemaphoreType.DMA((6,)),
        ],
        name="pack",
        compiler_params=pltpu.CompilerParams(vmem_limit_bytes=16 * 2**20),
    )(
        pltpu.with_memory_space_constraint(fields, pltpu.HBM),
        pltpu.with_memory_space_constraint(modes, pltpu.HBM),
    )


def up(x, axis):
    return pltpu.roll(x, x.shape[axis] - 1, axis)


def down(x, axis):
    return pltpu.roll(x, 1, axis)


def fluxes(u, directions):
    density, m1, m2, m3, energy = u
    half = 0.5 * TIME_STEP
    share = half / density
    momenta = (m1, m2, m3)
    v = [m * share for m in momenta]
    products = {(i, i): momenta[i] * v[i] for i in range(3)}
    squares = products[(0, 0)] + products[(1, 1)] + products[(2, 2)]
    pressure = (half * (GAMMA - 1.0)) * energy - (0.5 * (GAMMA - 1.0)) * squares
    total = energy + (1.0 / half) * pressure
    out = []
    for d in directions:
        row = [half * momenta[d]]
        for i in range(3):
            if i == d:
                row.append(products[(d, d)] + pressure)
            else:
                key = (min(i, d), max(i, d))
                if key not in products:
                    products[key] = momenta[key[0]] * v[key[1]]
                row.append(products[key])
        row.append(total * v[d])
        out.append(row)
    return out


CENTRE = 1.0 - 6.0 * VISCOSITY * TIME_STEP
SOFT = VISCOSITY * TIME_STEP


def across(u):
    flux = fluxes(u, (0,))[0]
    smooth = [SOFT * x for x in u]
    ahead = [smooth[c] - flux[c] for c in range(5)]
    behind = [smooth[c] + flux[c] for c in range(5)]
    return ahead, behind


def beside(above, below, edge, slot):
    edge[0, slot, 8 : 8 + NY] = above
    edge[0, slot, 8 + NY : 9 + NY] = above[0:1]
    edge[1, slot, 8 : 8 + NY] = below
    edge[1, slot, 7:8] = below[NY - 1 : NY]
    return edge[0, slot, 9 : 9 + NY] + edge[1, slot, 7 : 7 + NY]


def within(u, edge, slot):
    rows = fluxes(u, (0, 1, 2))
    smooth = [SOFT * x for x in u]
    ahead = [smooth[c] - rows[0][c] for c in range(5)]
    behind = [smooth[c] + rows[0][c] for c in range(5)]
    total = []
    for c in range(5):
        total.append(
            CENTRE * u[c]
            + beside(smooth[c] - rows[1][c], smooth[c] + rows[1][c], edge, 5 * slot + c)
            + (up(smooth[c] - rows[2][c], 1) + down(smooth[c] + rows[2][c], 1))
        )
    return ahead, behind, total


def joined(total, ahead, behind, after, before, lane):
    out = []
    for c in range(5):
        plus = pltpu.roll(ahead[c], 128 - WINDOW, 1)
        if after is not None:
            plus = jnp.where(lane < 2 * WINDOW, plus, pltpu.roll(after[c], 2 * WINDOW, 1))
        minus = pltpu.roll(behind[c], WINDOW, 1)
        if before is not None:
            minus = jnp.where(lane < WINDOW, pltpu.roll(before[c], 128 - 2 * WINDOW, 1), minus)
        out.append(total[c] + (plus + minus))
    return out


def section_all(load, lane, edge, slot):
    parts = []
    for g in range(3):
        parts.append(within(load(g), edge, slot + g))
        if g >= 1:
            ahead, behind, total = parts[g - 1]
            before = parts[g - 2][1] if g >= 2 else None
            yield g - 1, joined(total, ahead, behind, parts[g][0], before, lane)
    ahead, behind, total = parts[2]
    yield 2, joined(total, ahead, behind, None, parts[1][1], lane)


def step_kernel(w_ref, recv_ref, modes_ref, pair_ref, home_ref, base, one, two, turn_ref, edge):
    w = w_ref[0]
    lane = lanes((NY, 128))

    for g in range(3):
        planes = []
        places = []
        for j in range(3):
            start = lax.rem(w + (3 * g - 4 + j + WIDE), WIDE) * NARROW
            block = recv_ref[pl.ds(start, NARROW)].astype(F32)
            planes.append((block[:, 0:8].reshape(NY, 128), block[:, 8:16].reshape(NY, 128)))
            places.append((lane >= WINDOW * j) & (lane < WINDOW * (j + 1)))
        for c in range(5):
            moved = []
            for j in range(3):
                amount = WINDOW * (j - c % 3) % 128
                value = planes[j][c // 3]
                moved.append(pltpu.roll(value, amount, 1) if amount else value)
            value = jnp.where(places[0], moved[0], jnp.where(places[1], moved[1], moved[2]))
            at = 3 * WINDOW + c
            mean = [
                jnp.broadcast_to(planes[j][0][:, at : at + 1], (NY, 128)) for j in range(3)
            ]
            mean = jnp.where(places[0], mean[0], jnp.where(places[1], mean[1], mean[2]))
            base[g, c] = value + mean

    terms = recv_ref[:, 8:16, :].astype(F32)
    summed = jnp.sum(terms, axis=0)
    block = (pltpu.roll(summed, 16, 1) + pltpu.roll(summed, 32, 1)) + pltpu.roll(summed, 48, 1)

    packed = [jnp.zeros((NY, 128), F32) for _ in range(5)]

    def keep(index, u, out):
        for c in range(5):
            value = pltpu.roll(u[c], (ZPART * index - WINDOW - HALO) % 128, 1)
            inside = (lane >= ZPART * index) & (lane < ZPART * (index + 1))
            out[c] = jnp.where(inside, value, out[c])

    def stored(ref):
        return lambda g: [ref[g, c] for c in range(5)]

    for g, v in section_all(stored(base), lane, edge, 0):
        for c in range(5):
            one[g, c] = v[c]
        if g == 1:
            keep(0, v, packed)
    first, middle, last = [stored(one)(g) for g in range(3)]
    side = [jnp.where(lane < WINDOW, last[c], first[c]) for c in range(5)]
    side_ahead, side_behind, side_total = within(side, edge, 3)
    ahead, behind, total = within(middle, edge, 4)
    far_ahead = across(last)[0]
    v = joined(total, ahead, behind, side_ahead, side_behind, lane)
    new = [0.5 * (base[1, c] + v[c]) for c in range(5)]
    for c in range(5):
        two[1, c] = new[c]
    keep(1, new, packed)
    outer = []
    for c in range(5):
        plus = jnp.where(
            lane < WINDOW,
            pltpu.roll(far_ahead[c], 128 - WINDOW, 1),
            pltpu.roll(ahead[c], 2 * WINDOW, 1),
        )
        minus = jnp.where(
            lane < WINDOW,
            pltpu.roll(behind[c], 128 - 2 * WINDOW, 1),
            pltpu.roll(side_behind[c], WINDOW, 1),
        )
        held = jnp.where(lane < WINDOW, base[2, c], base[0, c])
        outer.append(0.5 * (held + (side_total[c] + (plus + minus))))
    after, before = across(outer)
    ahead, behind, total = within([two[1, c] for c in range(5)], edge, 6)
    third = joined(total, ahead, behind, after, before, lane)
    keep(2, third, packed)
    ahead, behind, total = within(third, edge, 7)
    fourth = joined(total, ahead, behind, None, None, lane)
    fourth = [0.5 * (two[1, c] + fourth[c]) for c in range(5)]
    keep(3, fourth, packed)
    change = [fourth[c] - base[1, c] for c in range(5)]
    spread = jnp.zeros((NY, 128), F32)
    for c in range(4):
        value = pltpu.roll(change[c], (ZPART * c - WINDOW - HALO) % 128, 1)
        inside = (lane >= ZPART * c) & (lane < ZPART * (c + 1))
        spread = jnp.where(inside, value, spread)
    home_ref[0] = spread
    home_ref[1] = pltpu.roll(change[4], 128 - WINDOW - HALO, 1)

    contract = (((1,), (1,)), ((), ()))
    for c in range(5):
        rounded = packed[c].astype(BF16).astype(F32)
        pair = jnp.concatenate([rounded, pltpu.roll(rounded, 127, 1)], axis=0)
        turn_ref[c] = pair.astype(BF16).T.astype(F32)
    chunks = [turn_ref[c, pl.ds(2 * k, 4, stride=ZPART), :] for c in range(5) for k in range(16)]
    rows = jnp.concatenate(chunks, axis=1).astype(BF16)
    every = jnp.concatenate([modes_ref[c] for c in range(5)], axis=1)
    cross = lax.dot_general(rows, every, contract, preferred_element_type=F32)
    square = lax.dot_general(rows, rows, contract, preferred_element_type=F32)
    top = jnp.concatenate([cross, square], axis=1) * INVERSE_CELLS
    lane8 = lanes((8, 128))
    block = block * INVERSE_CELLS
    high = block.astype(BF16).astype(F32)
    rest = block - high
    middle = rest.astype(BF16).astype(F32)
    addends = jnp.where(
        lane8 < 48,
        pltpu.roll(high, 32, 1),
        jnp.where(lane8 < 64, pltpu.roll(middle, 48, 1), pltpu.roll(rest - middle, 64, 1)),
    )
    addends = jnp.where((lane8 >= ZPART) & (lane8 < 80), addends, 0.0)
    odd = lax.rem(w, 2) == 1
    pair_ref[0:4] = top
    pair_ref[4:8] = jnp.zeros((4, 128), F32)
    pair_ref[8:16] = jnp.where(odd, pltpu.roll(addends, 48, 1), addends)


def steps(w, recv, modes):
    return pl.pallas_call(
        step_kernel,
        in_specs=[
            pl.BlockSpec(memory_space=pltpu.SMEM),
            pl.BlockSpec(memory_space=pltpu.VMEM),
            pl.BlockSpec(memory_space=pltpu.VMEM),
        ],
        out_specs=[
            pl.BlockSpec(memory_space=pltpu.VMEM),
            pl.BlockSpec(memory_space=pltpu.VMEM),
        ],
        out_shape=[
            jax.ShapeDtypeStruct((16, 128), F32),
            jax.ShapeDtypeStruct((2, NY, 128), F32),
        ],
        scratch_shapes=[
            pltpu.VMEM((3, 5, NY, 128), F32),
            pltpu.VMEM((3, 5, NY, 128), F32),
            pltpu.VMEM((2, 5, NY, 128), F32),
            pltpu.VMEM((5, 128, 128), F32),
            pltpu.VMEM((2, 40, NY + 16, 128), F32),
        ],
        name="steps",
        compiler_params=pltpu.CompilerParams(vmem_limit_bytes=24 * 2**20),
    )(w, recv, modes)


def merge_kernel(pair_ref, other_ref, home_ref, whole_ref):
    both = pair_ref[...] + other_ref[...]
    top = both[0:4]
    high = top.astype(BF16).astype(F32)
    first = jnp.concatenate([high, top - high], axis=0)
    lane8 = lanes((8, 128))
    for n in range(NARROW):
        rows = slice(YPART * n, YPART * (n + 1))
        third = jnp.where(lane8 < ZPART, home_ref[1, rows], both[8:16])
        piece = jnp.concatenate([first, home_ref[0, rows], third], axis=0).astype(BF16)
        whole_ref[:, n] = jnp.broadcast_to(piece[None], (CHIPS, 24, 128))


def merge(pair, other, home):
    return pl.pallas_call(
        merge_kernel,
        in_specs=[pl.BlockSpec(memory_space=pltpu.VMEM)] * 3,
        out_specs=pl.BlockSpec(memory_space=pltpu.VMEM),
        out_shape=jax.ShapeDtypeStruct((CHIPS, NARROW, 24, 128), BF16),
        name="merge",
        compiler_params=pltpu.CompilerParams(vmem_limit_bytes=16 * 2**20),
    )(pair, other, home)


def along_lanes(x, j):
    return jnp.broadcast_to(x[:, j : j + 1], x.shape)


def along_rows(x, i):
    return jnp.broadcast_to(x[i : i + 1, :], x.shape)


NEAR = 2


def tree(terms):
    terms = list(terms)
    while len(terms) > 1:
        terms = [
            terms[t] + terms[t + 1] if t + 1 < len(terms) else terms[t]
            for t in range(0, len(terms), 2)
        ]
    return terms[0]


def factor_rows(panels):
    panels = list(panels)
    lane = lanes((8, 128))
    row = lax.broadcasted_iota(jnp.int32, (8, 128), 0)
    count = len(panels)
    done = []
    for k in range(count):
        base = 8 * k
        near = range(k + 1, min(k + 1 + NEAR, count))
        far = range(k + 1 + NEAR, count)
        columns = [along_lanes(panels[k], base + j) for j in range(8)]
        rows = [along_rows(panels[k], i) for i in range(8)]
        below = {q: [along_lanes(panels[q], base + j) for j in range(8)] for q in near}
        scaled = []
        unit = []
        weights = {}
        for i in range(8):
            pivot = along_rows(columns[i], i)
            inverse = 1.0 / pivot
            for j in range(i + 1, 8):
                weight = along_rows(columns[j], i) * inverse
                weights[(i, j)] = weight
                columns[j] = columns[j] - columns[i] * weight
                rows[j] = rows[j] - rows[i] * weight
                for q in near:
                    below[q][j] = below[q][j] - below[q][i] * weight
            scaled.append(rows[i] * inverse)
            unit.append(rows[i] * lax.rsqrt(pivot))
        out = unit[7]
        for i in range(7):
            out = jnp.where(row == i, unit[i], out)
        done.append(jnp.where(lane >= row + base, out, 0.0))
        for q in near:
            panels[q] = panels[q] - tree(below[q][i] * scaled[i] for i in range(8))
        if len(far):
            answer = list(scaled)
            for i in range(6, -1, -1):
                answer[i] = scaled[i] - tree(
                    [weights[(i, j)] * answer[j] for j in range(7, i, -1)]
                )
            solved = answer[7]
            for i in range(7):
                solved = jnp.where(row == i, answer[i], solved)
            blank = jnp.zeros((8, 128), F32)
            factor = jnp.concatenate([blank] * k + [solved] + [blank] * (15 - k), axis=0)
            held = jnp.concatenate([panels[q] for q in far], axis=0)
            change = jnp.dot(
                held, factor, precision=lax.Precision.HIGHEST, preferred_element_type=F32
            )
            for t, q in enumerate(far):
                panels[q] = panels[q] - change[8 * t : 8 * t + 8]
    return done


def finish_kernel(w_ref, whole_ref, known_ref, factor_ref, state_ref):
    sums = jnp.sum(whole_ref[:, 0:8, :].astype(F32), axis=0)
    cross = sums[0:4] + sums[4:8]
    lane8 = lanes((8, 128))
    source = lax.broadcasted_iota(jnp.int32, (COLS, 256), 0)
    target = lanes((COLS, 256))
    start = ZPART + 48 * (target // 128)
    gram = jnp.zeros((CHIPS * 8, 256), F32)
    every = whole_ref[...].reshape(CHIPS, NARROW, 24, 128)[:, :, 16:24, :].astype(F32)
    for b in range(8):
        held = (source >= start) & (source < start + 48)
        match = target % 128 == 16 * b + source % 16
        chosen = jnp.where(held & match, 1.0, 0.0).astype(BF16)
        rows = every[:, b].reshape(CHIPS * 8, 128).astype(BF16)
        gram += jnp.dot(rows, chosen, preferred_element_type=F32)
    panels = []
    for a in range(16):
        m, core = a // 2, a % 2
        panels.append(gram[8 * m : 8 * m + 8, 128 * core : 128 * core + 128])
    panels[15] = jnp.concatenate([panels[15][0:4], cross], axis=0)
    turned = jnp.concatenate([panels[15]] * 16, axis=0).T
    for a in range(16):
        panels[a] = jnp.where(lane8 >= MODES, turned[8 * a : 8 * a + 8], panels[a])
    for a, rows in enumerate(factor_rows(panels)):
        factor_ref[8 * a : 8 * a + 8, :] = rows

    home = whole_ref[pl.ds(lax.div(w_ref[0], 2) * NARROW, NARROW), 8:24, :].astype(F32)
    lane = lanes((YPART, 256))
    for c in range(5):
        total = jnp.zeros((YPART, 256), F32)
        place = ZPART * (c % 4)
        row = 8 * (c // 4)
        for n in range(NARROW):
            part = home[n, row : row + 8, :]
            part = jnp.concatenate([part, part], axis=1)
            amount = (ZPART * n - place) % 256
            part = pltpu.roll(part, amount, 1) if amount else part
            inside = (lane >= ZPART * n) & (lane < ZPART * (n + 1))
            total = jnp.where(inside, part, total)
        state_ref[c] = known_ref[c] + total


def finish(w, whole, known):
    return pl.pallas_call(
        finish_kernel,
        in_specs=[
            pl.BlockSpec(memory_space=pltpu.SMEM),
            pl.BlockSpec(memory_space=pltpu.VMEM),
            pl.BlockSpec(memory_space=pltpu.VMEM),
        ],
        out_shape=[
            jax.ShapeDtypeStruct((COLS, 128), F32),
            jax.ShapeDtypeStruct((5, YPART, 256), F32),
        ],
        name="finish",
        compiler_params=pltpu.CompilerParams(vmem_limit_bytes=16 * 2**20),
    )(w, whole, known)


def local(fields, prior_modes):
    modes = jnp.transpose(prior_modes[:, :, 0, :], (1, 0, 2))
    w = lax.axis_index("wide").astype(jnp.int32).reshape(1)
    sent, modes, known = pack(fields[:, 0], modes)
    sent, w = lax.optimization_barrier((sent.reshape(DEVICES, 16, 128), w))
    recv = lax.all_to_all(sent, EVERYWHERE, split_axis=0, concat_axis=0, tiled=True)
    pair, home = steps(w, recv, modes)
    other = lax.ppermute(pair, "wide", [(i, i ^ 1) for i in range(WIDE)])
    whole = merge(pair, other, home).reshape(CHIPS * NARROW, 24, 128)
    groups = [
        [(2 * m + core) * NARROW + n for m in range(CHIPS) for n in range(NARROW)]
        for core in range(2)
    ]
    whole = lax.all_to_all(
        whole, EVERYWHERE, split_axis=0, concat_axis=0, axis_index_groups=groups, tiled=True
    )
    factor, state = finish(w, whole, known)
    return (state[:, None], factor)


def solution(mesh):
    placed = (P(None, "wide", "narrow", None), P(None, None, "wide", "narrow"))
    return jax.shard_map(
        local,
        mesh=mesh,
        in_specs=placed,
        out_specs=(P(None, "wide", "narrow", None), P()),
        check_vma=False,
    )
```
